256 devices in a mesh: tok: 32 (over x, y, core), feat: 8 (over z).
Axes of the slice: x: 4, y: 4, z: 8, core: 2. Of those that a mesh axis runs over, the one named last changes fastest.
Arguments:
- inputs: bfloat16 [16384, 2048], P(('tok', 'feat'))
- norm_gain: float32 [2048], replicated, may hold values from 0.1 to 1.9
- w_in: bfloat16 [512, 8192], P('tok', 'feat'), may hold values from -0.25 to 0.25
- w_out: bfloat16 [512, 8192], P('tok', 'feat'), may hold values from -0.125 to 0.125
- block_index: int32 [64, 4], P('feat'), may hold values from 0 to 15, all different within a row
- segment_ids: int32 [16384], P(('tok', 'feat')), may hold values from 0 to 1023, never falling along the last dimension, each value on 1 to 24 neighbouring positions
- teacher_scores: float32 [1024], replicated, may hold values from -6 to 6
- upstream: bfloat16 [16384, 2048], P(('tok', 'feat')), may hold values from -6 to 6
- readout: float32 [2048], replicated, may hold values from -0.125 to 0.125
Outputs:
- layer_out: bfloat16 [16384, 2048], P(('tok', 'feat'))
- input_grad: bfloat16 [16384, 2048], P(('tok', 'feat'))
- grad_in: float32 [512, 8192], P('tok', 'feat')
- grad_out: float32 [512, 8192], P('tok', 'feat')
The draws below stay inside these ranges and needn't reach their ends.
Inputs may be any that keep to these rules, and one draw needn't show every extreme that they name: `block_index`: each row names 4 different feature blocks; every feature block is named by some row. `segment_ids`: never falls along the tokens; every segment 0 to 1023 holds 1 to 24 tokens.
All inputs are finite; a program needn't handle non-finite values.
Results may differ from the reference program's by a relative error of at most 0.015.
Values may be sent and summed in bfloat16 or wider, within the bound.
A program may use at most 128 MiB of HBM per device.

```python
import math
import jax
import jax.numpy as jnp
import numpy as np
from jax import lax

D = 2048
FF = 8192
BLK = 128
SEG_MOST = 24
TOK_DEV = 64
KB = 4
TOKENS = 16384
NSEG = 1024
N_TOK = 32
N_FEAT = 8


def draw_inputs(key, part):
    first, second, third = jax.random.split(key, 3)
    base = jax.random.normal(first, (TOKENS, D), jnp.float32)
    row_scale = 0.5 * jnp.exp(jax.random.uniform(second, (TOKENS, 1), jnp.float32, 0.0, math.log(10.0)))
    col_scale = jnp.exp(jax.random.uniform(third, (1, D), jnp.float32, math.log(0.5), math.log(2.0)))
    return (base * row_scale * col_scale).astype(jnp.bfloat16)


def level_of(own_key, extent, cuts, smallest, top_value):
    loudness = 1.0
    for dim, blocks in cuts:
        steps = jax.random.uniform(jax.random.fold_in(jax.random.fold_in(own_key, 6), dim), (blocks,), jnp.float32, smallest / len(cuts), top_value / len(cuts))
        loudness = loudness * jnp.repeat(jnp.exp(steps), extent[dim] // blocks).reshape((-1,) + (1,) * (len(extent) - 1 - dim))
    return loudness


def different_ones(own_key, rows, amount, top, lift):
    sequence = jax.random.permutation(jax.random.fold_in(own_key, 1), amount)
    pull = sequence
    for power in range(3):
        pull = pull * pull // amount
    pull = pull * lift // amount
    lots = jax.random.randint(jax.random.fold_in(own_key, 2), (rows, amount), 0, 4096) + pull
    holders = jax.random.permutation(jax.random.fold_in(own_key, 3), rows)[jnp.arange(amount) % rows]
    lots = jnp.where(jnp.arange(rows)[:, None] == holders[None, :], 1 << 14, lots)
    merit = lots * amount + jnp.arange(amount)
    return lax.top_k(merit.astype(jnp.int32), top)[1].astype(jnp.int32)


def profile(amount, total, bound, skew):
    loads = [(1 << 20) // math.isqrt(standing ** skew) + 1 for standing in range(2, amount + 1)]
    rest, given = total - bound - (amount - 1), [1] * (amount - 1)
    while rest > 0:
        movable = [i for i in range(amount - 1) if given[i] < bound]
        whole, budget = sum([loads[i] for i in movable]), rest
        for i in movable:
            more = min(bound - given[i], max(1, budget * loads[i] // whole), rest)
            given[i] = given[i] + more
            rest = rest - more
    return np.array([bound] + given)


def uneven_parts(stream_key, amount, total, most, skew):
    if amount == 2:
        one = jax.random.randint(stream_key, (), max(1, total - most), min(most, total - 1) + 1)
        return jnp.stack([one, total - one])
    tallies = jnp.asarray(profile(amount, total, most, skew), jnp.int32)
    pairs = (amount - 1) // 2
    donor, sink = tallies[1:1 + 2 * pairs:2], tallies[2:2 + 2 * pairs:2]
    slack = jnp.minimum(donor - 1, most - sink)
    passed = jax.random.randint(jax.random.fold_in(stream_key, 1), (pairs,), 0, 1 << 20) % (slack + 1)
    tallies = tallies.at[1:1 + 2 * pairs:2].set(donor - passed).at[2:2 + 2 * pairs:2].set(sink + passed)
    return tallies[jax.random.permutation(jax.random.fold_in(stream_key, 2), amount)]


def bell_draw(key, dims, deviation, reach, cuts=(), held_as=jnp.bfloat16):
    entries = deviation * jax.random.normal(key, dims, jnp.float32)
    if cuts:
        entries = entries * level_of(key, dims, cuts, -0.22, 0.18)
    return jnp.clip(entries, -reach, reach).astype(held_as)


def setup_inputs(seed: int = 0) -> dict:
    key_of = jax.random.split(jax.random.key(seed), 10)
    return {
        "inputs": draw_inputs(jax.random.fold_in(key_of[9], 71), 0),
        "norm_gain": jnp.clip(1.0 + 0.18 * jax.random.normal(key_of[1], (D,), jnp.float32), 0.1, 1.9),
        "w_in": bell_draw(key_of[2], (KB * BLK, FF), (KB * BLK) ** -0.5, 0.25, ((0, 32), (1, 8))),
        "w_out": bell_draw(key_of[3], (KB * BLK, FF), (FF * KB // (D // BLK)) ** -0.5, 0.125, ((0, 32), (1, 8))),
        "block_index": different_ones(key_of[4], (FF // BLK), D // BLK, KB, 2048),
        "segment_ids": jnp.searchsorted(jnp.cumsum(uneven_parts(key_of[5], NSEG, TOKENS, SEG_MOST, 1)), jnp.arange(TOKENS), side="right").astype(jnp.int32),
        "teacher_scores": bell_draw(key_of[6], (NSEG,), 1.0, 6.0, (), jnp.float32),
        "upstream": bell_draw(key_of[7], (TOKENS, D), 1.0, 6.0, ((0, 256),)),
        "readout": bell_draw(key_of[8], (D,), D ** -0.5, 0.125, (), jnp.float32),
    }


EPS = 1e-06
LOSS_WEIGHT = 8.0
HIGHEST = lax.Precision.HIGHEST

def gelu_tanh(values):
    return jax.nn.gelu(values, approximate=True)

def gelu_back(values, cotangent):
    return jax.vjp(gelu_tanh, values)[1](cotangent)[0]

def rounded(values):
    return lax.optimization_barrier(values.astype(jnp.bfloat16)).astype(jnp.float32)

def reference(inputs, norm_gain, w_in, w_out, block_index, segment_ids, teacher_scores, upstream, readout):
    feature_blocks = D // BLK
    hidden_blocks = FF // BLK
    group_blocks = hidden_blocks // N_FEAT
    picked_width = KB * BLK
    group_rows = TOK_DEV * N_FEAT
    selector = (block_index[:, :, None] == jnp.arange(feature_blocks, dtype=jnp.int32)[None, None, :]).astype(jnp.float32)
    sel_groups = selector.reshape(N_FEAT, group_blocks, KB, feature_blocks)
    w_in_blocks = w_in.astype(jnp.float32).reshape(picked_width, hidden_blocks, BLK)
    w_out_blocks = w_out.astype(jnp.float32).reshape(picked_width, hidden_blocks, BLK)
    inputs_wide = inputs.astype(jnp.float32)
    inv_rms = lax.rsqrt(lax.optimization_barrier(jnp.mean(inputs_wide * inputs_wide, axis=1, keepdims=True)) + EPS)
    normed = (inputs_wide * inv_rms * norm_gain[None, :]).astype(jnp.bfloat16)

    def select(rows):
        blocks = rows.astype(jnp.float32).reshape(group_rows, feature_blocks, BLK)
        picked = jnp.einsum('rdc,jkd->rjkc', blocks, selector, precision=HIGHEST)
        return picked.reshape(group_rows, hidden_blocks, picked_width)

    def spread(terms):
        grouped = terms.reshape(group_rows, N_FEAT, group_blocks, KB, BLK)
        parts = jnp.einsum('rgjkc,gjkd->rgdc', grouped, sel_groups, precision=HIGHEST)
        return lax.optimization_barrier(jnp.sum(rounded(parts), axis=1)).reshape(group_rows, D)

    def forward_group(rows):
        pre_act = jnp.einsum('rjm,mjc->rjc', select(rows), w_in_blocks, precision=HIGHEST)
        activated = rounded(gelu_tanh(pre_act))
        terms = jnp.einsum('rjc,mjc->rjm', activated, w_out_blocks, precision=HIGHEST)
        return spread(terms)
    normed_groups = normed.reshape(N_TOK, group_rows, D)
    branch = lax.map(forward_group, normed_groups).reshape(TOKENS, D)
    layer_out = (inputs_wide + branch).astype(jnp.bfloat16)
    token_score = jnp.dot(layer_out.astype(jnp.float32), readout, precision=HIGHEST)
    score_sums = jax.ops.segment_sum(token_score, segment_ids, num_segments=NSEG)
    token_counts = jax.ops.segment_sum(jnp.ones_like(token_score), segment_ids, num_segments=NSEG)
    misfit = score_sums / token_counts - teacher_scores
    token_coeff = 2.0 * LOSS_WEIGHT * misfit[segment_ids]
    cotangent = (upstream.astype(jnp.float32) + token_coeff[:, None] * readout[None, :]).astype(jnp.bfloat16)

    def backward_group(totals, items):
        rows, grads = items
        chosen = select(rows)
        pre_act = jnp.einsum('rjm,mjc->rjc', chosen, w_in_blocks, precision=HIGHEST)
        activated = rounded(gelu_tanh(pre_act))
        chosen_grad = select(grads)
        upper_grad = jnp.einsum('rjm,mjc->rjc', chosen_grad, w_out_blocks, precision=HIGHEST)
        pre_grad = rounded(gelu_back(pre_act, upper_grad))
        back_terms = jnp.einsum('rjc,mjc->rjm', pre_grad, w_in_blocks, precision=HIGHEST)
        in_terms = jnp.einsum('rjm,rjc->mjc', chosen, pre_grad, precision=HIGHEST)
        out_terms = jnp.einsum('rjm,rjc->mjc', chosen_grad, activated, precision=HIGHEST)
        return ((totals[0] + in_terms, totals[1] + out_terms), spread(back_terms))
    zero_grads = jnp.zeros((picked_width, hidden_blocks, BLK), jnp.float32)
    cot_groups = cotangent.reshape(N_TOK, group_rows, D)
    (in_total, out_total), back = lax.scan(backward_group, (zero_grads, zero_grads), (normed_groups, cot_groups))
    back = back.reshape(TOKENS, D)
    scaled = back * norm_gain[None, :]
    inner_mean = lax.optimization_barrier(jnp.mean(scaled * inputs_wide, axis=1, keepdims=True))
    norm_back = inv_rms * scaled - inputs_wide * (inv_rms * inv_rms * inv_rms) * inner_mean
    input_grad = (cotangent.astype(jnp.float32) + norm_back).astype(jnp.bfloat16)
    grad_scale = 1.0 / math.sqrt(TOKENS)
    grad_in = in_total.reshape(picked_width, FF) * grad_scale
    grad_out = out_total.reshape(picked_width, FF) * grad_scale
    return (layer_out, input_grad, grad_in, grad_out)
```

```python
import functools
import heapq
import math

import jax
import jax.numpy as jnp
from jax import lax
from jax.experimental import pallas as pl
from jax.experimental.pallas import tpu as pltpu
from jax.sharding import PartitionSpec as P

BLK = 128
EPS = 1e-06
LOSS_WEIGHT = 8.0
X, Y, C, Z = 4, 4, 2, 8
Q = Y * C
ROWS = 64
WIDTH = 2048
KB = 4
MESH = pl.DeviceIdType.MESH
F32, BF16 = jnp.float32, jnp.bfloat16
NT = (((1,), (1,)), ((), ()))
NN = (((1,), (0,)), ((), ()))
VM = pl.BlockSpec(memory_space=pltpu.VMEM)
ANY = pl.BlockSpec(memory_space=pl.ANY)


def dot(a, b, dims):
    return lax.dot_general(a, b, dims, preferred_element_type=F32)


class Place:
    def __init__(self):
        t = lax.axis_index("tok")
        self.z = lax.axis_index("feat")
        self.t = t
        self.q = lax.rem(t, Q)
        self.c = lax.rem(t, C)
        self.y = lax.rem(t // C, Y)
        self.x = t // Q

    def at(self, x=None, y=None, c=None, z=None):
        x, y = self.x if x is None else x, self.y if y is None else y
        c, z = self.c if c is None else c, self.z if z is None else z
        return {"tok": (x * Y + y) * C + c, "feat": z}

    def sibling(self):
        return self.at(c=1 - self.c)

    def along(self, axis, by):
        n = {"x": X, "y": Y, "z": Z}[axis]
        me = {"x": self.x, "y": self.y, "z": self.z}[axis]
        return self.at(**{axis: lax.rem(me + by + n, n)})

    def member(self, by):
        return {"tok": self.x * Q + lax.rem(self.q + by + Q, Q), "feat": self.z}

    def flat(self, by):
        n = X * Q * Z
        d = lax.rem(self.t * Z + self.z + by + n, n)
        return {"tok": d // Z, "feat": lax.rem(d, Z)}


class Mail:
    def __init__(self, send_sem, recv_sem):
        self.send_sem, self.recv_sem, self.sent = send_sem, recv_sem, []

    def send(self, src, dst, to):
        i = len(self.sent)
        copy = pltpu.make_async_remote_copy(
            src_ref=src,
            dst_ref=dst,
            send_sem=self.send_sem.at[i],
            recv_sem=self.recv_sem.at[i],
            device_id=to,
            device_id_type=MESH,
        )
        copy.start()
        self.sent.append(copy)
        return copy

    def close(self):
        for copy in self.sent:
            copy.wait_send()


def greet(devices):
    barrier = pltpu.get_barrier_semaphore()
    for device in devices:
        pl.semaphore_signal(barrier, inc=1, device_id=device, device_id_type=MESH)
    pl.semaphore_wait(barrier, len(devices))


class Flows:
    def __init__(self):
        self.heap, self.now, self.count = [], 0.0, 0

    def add(self, flow):
        heapq.heappush(self.heap, (self.now, self.count, flow))
        self.count += 1

    def run(self):
        while self.heap:
            self.now, _, flow = heapq.heappop(self.heap)
            for delay in flow:
                heapq.heappush(self.heap, (self.now + delay, self.count, flow))
                self.count += 1
                break


def gather_ring(mail, n, me, plus, minus, piece, half, delays, arrived=None):
    a = mail.send(piece(me), piece(me), plus)
    b = mail.send(piece(me), piece(me), minus)
    for step in range(1, n // 2 + 1):
        yield delays[step - 1]
        last = step == n // 2
        a.wait_recv()
        left = lax.rem(me - step + n, n)
        if not last:
            ref = half(left, 0) if step == n // 2 - 1 else piece(left)
            a = mail.send(ref, ref, plus)
            if arrived:
                arrived(left, None)
        elif arrived:
            arrived(left, 0)
        b.wait_recv()
        right = lax.rem(me + step, n)
        if not last:
            ref = half(right, 1) if step == n // 2 - 1 else piece(right)
            b = mail.send(ref, ref, minus)
            if arrived:
                arrived(right, None)
        elif arrived:
            arrived(right, 1)


def reduce_ring(mail, n, me, plus, minus, own, half, full, stage, land, delays, done):
    steps = n // 2
    far = lax.rem(me + steps, n)
    a = mail.send(half(own(far), 0), half(land(0, 1), 0), plus)
    b = mail.send(half(own(far), 1), half(land(1, 1), 1), minus)
    for step in range(2, steps + 1):
        yield delays[step - 2]
        for way in (0, 1):
            (a, b)[way].wait_recv()
            dest = lax.rem(me + steps - step + 1, n) if way == 0 else lax.rem(me - steps + step - 1 + n, n)
            mine, came, out = own(dest), land(way, step - 1), stage(way, step)
            if step == 2:
                half(out, way)[...] = (half(mine, way)[...].astype(F32) + half(came, way)[...].astype(F32)).astype(BF16)
                half(out, 1 - way)[...] = half(mine, 1 - way)[...]
            else:
                out[...] = (mine[...].astype(F32) + came[...].astype(F32)).astype(BF16)
            sent = mail.send(out, land(way, step), plus if way == 0 else minus)
            if way == 0:
                a = sent
            else:
                b = sent
    yield delays[steps - 1]
    a.wait_recv()
    b.wait_recv()
    done(own(me)[...].astype(F32) + land(0, steps)[...].astype(F32) + land(1, steps)[...].astype(F32))


def gather_kernel(x_ref, up_ref, gain_ref, win_ref, wout_ref, bi_ref,
                  nrm_all, up_all, win_all, wout_all, bi_all,
                  nrm_v, send_sem, recv_sem, local_sem):
    p = Place()
    mail = Mail(send_sem, recv_sem)
    ring = [p.along(a, s) for a in "xz" for s in (-1, 1)]
    greet([p.member(o) for o in range(1, Q)] + ring[:2] + [p.along("z", o) for o in range(1, Z)])
    local = []

    def keep(src, dst):
        copy = pltpu.make_async_copy(src, dst, local_sem.at[len(local)])
        copy.start()
        local.append(copy)

    flows = Flows()

    def columns(ref, q):
        return ref.at[:, pl.ds(pl.multiple_of(q * BLK, BLK), BLK)]

    def my_rows(ref):
        return ref.at[pl.ds(pl.multiple_of(p.q * 16, 16), 16), :]

    in_slab, out_slab = win_all.at[p.z, p.x], wout_all.at[p.x, p.z]
    deals = []
    for o in range(1, Q):
        to, q = p.member(o), lax.rem(p.q + o, Q)
        deals.append(mail.send(columns(win_ref, q), my_rows(in_slab), to))
        deals.append(mail.send(columns(wout_ref, q), my_rows(out_slab), to))
    keep(columns(win_ref, p.q), my_rows(in_slab))
    keep(columns(wout_ref, p.q), my_rows(out_slab))
    slab_copies = list(local)
    tables = [mail.send(bi_ref, bi_all.at[p.z], p.along("z", o)) for o in range(1, Z)]
    keep(bi_ref, bi_all.at[p.z])

    def tokens(own, out, first):
        def piece(y):
            return out.at[y * C + p.c]

        def half(y, h):
            return out.at[y * C + p.c, pl.ds(h * 32, 32), :]

        relays = []

        def arrived(y, h):
            ref = piece(y) if h is None else half(y, h)
            relays.append(mail.send(ref, ref, p.sibling()))

        plus, minus = p.along("y", 1), p.along("y", -1)
        mine = out.at[p.q]
        a = mail.send(own, mine, plus)
        b = mail.send(own, mine, minus)
        relays.append(mail.send(own, mine, p.sibling()))
        keep(own, mine)
        yield first
        left, right = lax.rem(p.y + 3, Y), lax.rem(p.y + 1, Y)
        a.wait_recv()
        a = mail.send(half(left, 0), half(left, 0), plus)
        arrived(left, None)
        b.wait_recv()
        b = mail.send(half(right, 1), half(right, 1), minus)
        arrived(right, None)
        yield 5.0
        far = lax.rem(p.y + 2, Y)
        a.wait_recv()
        arrived(far, 0)
        b.wait_recv()
        arrived(far, 1)
        yield 5.0
        for copy in relays:
            copy.wait_recv()

    flows.add(tokens(up_ref, up_all, 10.0))
    xf = x_ref[...].astype(F32)
    inv = lax.rsqrt(jnp.mean(xf * xf, axis=1, keepdims=True) + EPS)
    nrm_v[...] = (xf * inv * gain_ref[...]).astype(BF16)
    flows.add(tokens(nrm_v, nrm_all, 9.5))

    xplus, xminus = p.along("x", 1), p.along("x", -1)
    zplus, zminus = p.along("z", 1), p.along("z", -1)
    slow, quick = [2.5] * 4, [2.0] * 4

    def w_in_z(k):
        return gather_ring(
            mail, Z, p.z, zplus, zminus,
            lambda z: win_all.at[z, k],
            lambda z, h: win_all.at[z, k, pl.ds(h * 64, 64), :],
            [3.5] * 4)

    def w_out_x(z):
        return gather_ring(
            mail, X, p.x, xplus, xminus,
            lambda x: wout_all.at[x, z],
            lambda x, h: wout_all.at[x, z, pl.ds(h * 64, 64), :],
            [3.5] * 4)

    def weights():
        yield 2.5
        for copy in deals:
            copy.wait_recv()
        for copy in slab_copies:
            copy.wait()

        parts = {}

        def got(x, h):
            if h is None:
                flows.add(w_in_z(x))
            else:
                parts[h] = True
                if len(parts) == 2:
                    flows.add(w_in_z(x))

        both = {}

        def got_out(z, h):
            if h is None:
                flows.add(w_out_x(z))
            else:
                both[h] = True
                if len(both) == 2:
                    flows.add(w_out_x(z))

        flows.add(gather_ring(
            mail, X, p.x, xplus, xminus,
            lambda x: win_all.at[p.z, x],
            lambda x, h: win_all.at[p.z, x, pl.ds(h * 64, 64), :],
            quick, got))
        flows.add(gather_ring(
            mail, Z, p.z, zplus, zminus,
            lambda z: wout_all.at[p.x, z],
            lambda z, h: wout_all.at[p.x, z, pl.ds(h * 64, 64), :],
            quick, got_out))
        flows.add(w_in_z(p.x))
        flows.add(w_out_x(p.z))

    flows.add(weights())
    flows.run()
    for copy in tables:
        copy.wait_recv()
    for copy in local[len(slab_copies):]:
        copy.wait()
    mail.close()


def gather_all(x, up, gain, w_in, w_out, table):
    return pl.pallas_call(
        gather_kernel,
        name="gather_all",
        out_shape=(
            jax.ShapeDtypeStruct((Q, ROWS, WIDTH), BF16),
            jax.ShapeDtypeStruct((Q, ROWS, WIDTH), BF16),
            jax.ShapeDtypeStruct((Z, KB, BLK, BLK), BF16),
            jax.ShapeDtypeStruct((KB, Z, BLK, BLK), BF16),
            jax.ShapeDtypeStruct((Z, 8, BLK), jnp.int32),
        ),
        in_specs=[VM] * 6,
        out_specs=(ANY,) * 5,
        scratch_shapes=[
            pltpu.VMEM((ROWS, WIDTH), BF16),
            pltpu.SemaphoreType.DMA((128,)),
            pltpu.SemaphoreType.DMA((128,)),
            pltpu.SemaphoreType.DMA((8,)),
        ],
        compiler_params=pltpu.CompilerParams(collective_id=0, has_side_effects=True),
    )(x, up, gain, w_in, w_out, table)


SQ = math.sqrt(2.0 / math.pi)


def forward_kernel(bi_ref, nrm_ref, win_ref, wout_ref, part_ref, act_ref, slope_ref, acc):
    q = lax.rem(lax.axis_index("tok"), Q)
    acc[...] = jnp.zeros_like(acc)

    def block(j, carry):
        at = [pl.multiple_of(bi_ref[j, q, k] * BLK, BLK) for k in range(KB)]
        picked = jnp.concatenate([nrm_ref[:, pl.ds(a, BLK)] for a in at], axis=1)
        v = dot(picked, win_ref[j].reshape(KB * BLK, BLK), NN)
        tanh = jnp.tanh(SQ * (v + 0.044715 * (v * v * v)))
        act = 0.5 * v * (1.0 + tanh)
        slope = 0.5 * (1.0 + tanh) + 0.5 * v * (1.0 - tanh * tanh) * (SQ * (1.0 + 3.0 * 0.044715 * (v * v)))
        act_half = act.astype(BF16)
        act_ref[j] = act.T.astype(BF16)
        slope_ref[j] = slope
        for k in range(KB):
            acc[:, pl.ds(at[k], BLK)] += dot(act_half, wout_ref[k, j], NT)
        return carry

    lax.fori_loop(0, Z, block, 0)
    part_ref[...] = acc[...].astype(BF16)


def forward(table, nrm, w_in, w_out):
    n = Q * ROWS
    return pl.pallas_call(
        forward_kernel,
        name="forward",
        out_shape=(
            jax.ShapeDtypeStruct((n, WIDTH), BF16),
            jax.ShapeDtypeStruct((Z, BLK, n), BF16),
            jax.ShapeDtypeStruct((Z, n, BLK), F32),
        ),
        in_specs=[pl.BlockSpec(memory_space=pltpu.SMEM), VM, VM, VM],
        out_specs=(VM,) * 3,
        scratch_shapes=[pltpu.VMEM((n, WIDTH), F32)],
    )(table, nrm, w_in, w_out)


def halves(ref, h):
    return ref.at[pl.ds(h * 32, 32), :]


def reduce_tokens(mail, p, part, rs, pair, stage, land, done, times):
    other = 1 - p.c
    order = [2, 1, 3, 0]
    sends = {}
    for o in order:
        y = lax.rem(p.y + o, Y)
        sends[o] = mail.send(part.at[y * C + other], rs.at[y], p.sibling())
    yield times[0]

    def fold(o):
        y = lax.rem(p.y + o, Y)
        sends[o].wait_recv()
        pair[y] = (part[y * C + p.c].astype(F32) + rs[y].astype(F32)).astype(BF16)

    fold(2)
    plus, minus = p.along("y", 1), p.along("y", -1)
    flow = reduce_ring(
        mail, Y, p.y, plus, minus,
        lambda y: pair.at[y], halves, None,
        lambda way, step: stage.at[way],
        lambda way, step: land.at[way, step - 1],
        times[1:], done)
    delay = next(flow)
    fold(1)
    fold(3)
    fold(0)
    yield delay
    yield from flow


def branch_kernel(part_ref, x_ref, seg_ref, teacher_ref, readout_ref,
                  lo_ref, coeff_ref,
                  rs, pair, stage, land, ids, scores, send_sem, recv_sem):
    p = Place()
    mail = Mail(send_sem, recv_sem)
    near = [p.flat(1), p.flat(-1)]
    greet([p.member(o) for o in range(1, Q)] + near)
    ids[0] = seg_ref[...]
    id_copies = [mail.send(ids.at[0], ids.at[1 + i], near[i]) for i in (0, 1)]
    total = []
    flows = Flows()
    flows.add(reduce_tokens(mail, p, part_ref, rs, pair, stage, land, total.append, [1.0, 4.0, 4.0]))
    eye = lax.broadcasted_iota(jnp.int32, (ROWS, BLK), 0) == lax.broadcasted_iota(jnp.int32, (ROWS, BLK), 1)
    ids_col = jnp.sum(jnp.where(eye, seg_ref[0:1, :], 0.0), axis=1, keepdims=True)
    segs = teacher_ref.shape[1]
    hot = lax.broadcasted_iota(jnp.int32, (ROWS, segs), 1).astype(F32) == ids_col
    teacher = jnp.sum(jnp.where(hot, teacher_ref[...], 0.0), axis=1, keepdims=True)
    flows.run()
    lo = (x_ref[...].astype(F32) + total[0]).astype(BF16)
    lo_ref[...] = lo
    score = jnp.sum(lo.astype(F32) * readout_ref[...], axis=1, keepdims=True)
    score_row = jnp.sum(jnp.where(eye, score, 0.0), axis=0, keepdims=True)
    scores[0] = jnp.broadcast_to(score_row, (8, BLK))
    copies = [mail.send(scores.at[0], scores.at[1 + i], near[i]) for i in (0, 1)]
    for copy in id_copies + copies:
        copy.wait_recv()
    sums = jnp.zeros((ROWS, 1), F32)
    counts = jnp.zeros((ROWS, 1), F32)
    for i in range(3):
        same = ids[i, 0:1, :] == ids_col
        sums += jnp.sum(jnp.where(same, scores[i, 0:1, :], 0.0), axis=1, keepdims=True)
        counts += jnp.sum(jnp.where(same, 1.0, 0.0), axis=1, keepdims=True)
    coeff = (2.0 * LOSS_WEIGHT) * (sums / counts - teacher)
    coeff_row = jnp.sum(jnp.where(eye, coeff, 0.0), axis=0, keepdims=True)
    coeff_ref[p.q] = jnp.broadcast_to(coeff_row, (8, BLK))
    out = [mail.send(coeff_ref.at[p.q], coeff_ref.at[p.q], p.member(o)) for o in range(1, Q)]
    for copy in out:
        copy.wait_recv()
    mail.close()


def branch_sum(part, x, seg, teacher, readout):
    return pl.pallas_call(
        branch_kernel,
        name="branch_sum",
        out_shape=(
            jax.ShapeDtypeStruct((ROWS, WIDTH), BF16),
            jax.ShapeDtypeStruct((Q, 8, BLK), F32),
        ),
        in_specs=[VM] * 5,
        out_specs=(VM,) * 2,
        scratch_shapes=[
            pltpu.VMEM((Y, ROWS, WIDTH), BF16),
            pltpu.VMEM((Y, ROWS, WIDTH), BF16),
            pltpu.VMEM((2, ROWS, WIDTH), BF16),
            pltpu.VMEM((2, 2, ROWS, WIDTH), BF16),
            pltpu.VMEM((3, 8, BLK), F32),
            pltpu.VMEM((3, 8, BLK), F32),
            pltpu.SemaphoreType.DMA((32,)),
            pltpu.SemaphoreType.DMA((32,)),
        ],
        compiler_params=pltpu.CompilerParams(collective_id=1, has_side_effects=True),
    )(part, x, seg, teacher, readout)


def backward_kernel(bi_ref, up_ref, coeff_ref, readout_ref, nrm_ref, win_ref, wout_ref, act_ref, slope_ref,
                    back_ref, din_ref, dout_ref, cot, acc):
    q = lax.rem(lax.axis_index("tok"), Q)
    acc[...] = jnp.zeros_like(acc)
    eye = lax.broadcasted_iota(jnp.int32, (ROWS, BLK), 0) == lax.broadcasted_iota(jnp.int32, (ROWS, BLK), 1)

    def form(b, carry):
        rows = pl.ds(pl.multiple_of(b * ROWS, ROWS), ROWS)
        coeff = jnp.sum(jnp.where(eye, coeff_ref[b][0:1, :], 0.0), axis=1, keepdims=True)
        cot[rows, :] = (up_ref[rows, :].astype(F32) + coeff * readout_ref[...]).astype(BF16)
        return carry

    lax.fori_loop(0, Q, form, 0)

    def block(j, carry):
        at = [pl.multiple_of(bi_ref[j, q, k] * BLK, BLK) for k in range(KB)]
        picked = jnp.concatenate([cot[:, pl.ds(a, BLK)] for a in at], axis=1)
        w_out = jnp.concatenate([wout_ref[k, j] for k in range(KB)], axis=0)
        upper = dot(picked, w_out, NN)
        pre = upper * slope_ref[j]
        pre_half = pre.astype(BF16)
        pre_t = pre.T.astype(BF16)
        act_t = act_ref[j]
        for k in range(KB):
            cols = pl.ds(at[k], BLK)
            acc[:, cols] += dot(pre_half, win_ref[j, k], NT)
            din_ref[j, k] = dot(pre_t, nrm_ref[:, cols], NN).astype(BF16)
            dout_ref[k, j] = dot(act_t, cot[:, cols], NN).astype(BF16)
        return carry

    lax.fori_loop(0, Z, block, 0)
    back_ref[...] = acc[...].astype(BF16)


def backward(table, up, coeff, readout, nrm, w_in, w_out, act, slope):
    n = Q * ROWS
    return pl.pallas_call(
        backward_kernel,
        name="backward",
        out_shape=(
            jax.ShapeDtypeStruct((n, WIDTH), BF16),
            jax.ShapeDtypeStruct((Z, KB, BLK, BLK), BF16),
            jax.ShapeDtypeStruct((KB, Z, BLK, BLK), BF16),
        ),
        in_specs=[pl.BlockSpec(memory_space=pltpu.SMEM)] + [VM] * 8,
        out_specs=(VM,) * 3,
        scratch_shapes=[pltpu.VMEM((n, WIDTH), BF16), pltpu.VMEM((n, WIDTH), F32)],
    )(table, up, coeff, readout, nrm, w_in, w_out, act, slope)


def rows64(ref, h):
    return ref.at[pl.ds(h * 64, 64), :]


def finish_kernel(scale, back_ref, din_ref, dout_ref, x_ref, up_ref, coeff_ref, readout_ref, gain_ref,
                  ig_ref, gin_ref, gout_ref,
                  rs, pair, stage, land,
                  za_stage, za_land, za_sum, xa_stage, xa_land,
                  xb_stage, xb_land, xb_sum, zb_stage, zb_land,
                  slab, dealt, send_sem, recv_sem):
    p = Place()
    mail = Mail(send_sem, recv_sem)
    greet([p.member(o) for o in range(1, Q)] + [p.along(a, s) for a in "xz" for s in (-1, 1)])
    flows = Flows()
    total = []
    flows.add(reduce_tokens(mail, p, back_ref, rs, pair, stage, land, total.append, [1.0, 8.0, 8.0]))
    xplus, xminus = p.along("x", 1), p.along("x", -1)
    zplus, zminus = p.along("z", 1), p.along("z", -1)
    deals = []

    def deal(w):
        def done(value):
            slab[w] = (value * scale).T.astype(BF16)
            dealt[w, p.q] = slab[w, pl.ds(pl.multiple_of(p.q * 16, 16), 16), :]
            for o in range(1, Q):
                q = lax.rem(p.q + o, Q)
                rows = slab.at[w, pl.ds(pl.multiple_of(q * 16, 16), 16), :]
                deals.append(mail.send(rows, dealt.at[w, p.q], p.member(o)))
        return done

    left = [KB]

    def in_z(k):
        def done(value):
            za_sum[k] = value.astype(BF16)
            left[0] -= 1
            if left[0] == 0:
                flows.add(reduce_ring(
                    mail, X, p.x, xplus, xminus,
                    lambda x: za_sum.at[x], rows64, None,
                    lambda way, step: xa_stage.at[way], lambda way, step: xa_land.at[way, step - 1],
                    [2.0] * 4, deal(0)))
        return reduce_ring(
            mail, Z, p.z, zplus, zminus,
            lambda z: din_ref.at[z, k], rows64, None,
            lambda way, step: za_stage.at[k, way, step - 2], lambda way, step: za_land.at[k, way, step - 1],
            [3.0] * 4, done)

    rest = [Z]

    def out_x(z):
        def done(value):
            xb_sum[z] = value.astype(BF16)
            rest[0] -= 1
            if rest[0] == 0:
                flows.add(reduce_ring(
                    mail, Z, p.z, zplus, zminus,
                    lambda z: xb_sum.at[z], rows64, None,
                    lambda way, step: zb_stage.at[way, step - 2], lambda way, step: zb_land.at[way, step - 1],
                    [2.0] * 4, deal(1)))
        return reduce_ring(
            mail, X, p.x, xplus, xminus,
            lambda x: dout_ref.at[x, z], rows64, None,
            lambda way, step: xb_stage.at[z, way], lambda way, step: xb_land.at[z, way, step - 1],
            [5.0] * 4, done)

    for i in range(KB):
        flows.add(in_z(i))
        flows.add(out_x(2 * i))
        flows.add(out_x(2 * i + 1))
    flows.run()

    xf = x_ref[...].astype(F32)
    inv = lax.rsqrt(jnp.mean(xf * xf, axis=1, keepdims=True) + EPS)
    eye = lax.broadcasted_iota(jnp.int32, (ROWS, BLK), 0) == lax.broadcasted_iota(jnp.int32, (ROWS, BLK), 1)
    coeff = jnp.sum(jnp.where(eye, coeff_ref[p.q][0:1, :], 0.0), axis=1, keepdims=True)
    cot = (up_ref[...].astype(F32) + coeff * readout_ref[...]).astype(BF16).astype(F32)
    scaled = total[0] * gain_ref[...]
    inner = jnp.mean(scaled * xf, axis=1, keepdims=True)
    ig_ref[...] = (cot + (inv * scaled - xf * (inv * inv * inv) * inner)).astype(BF16)
    for copy in deals:
        copy.wait_recv()
    for q in range(Q):
        gin_ref[:, q * BLK:(q + 1) * BLK] = dealt[0, q].astype(F32)
        gout_ref[:, q * BLK:(q + 1) * BLK] = dealt[1, q].astype(F32)
    mail.close()


def finish(scale, back, din, dout, x, up, coeff, readout, gain):
    tile = (BLK, BLK)
    return pl.pallas_call(
        functools.partial(finish_kernel, scale),
        name="finish",
        out_shape=(
            jax.ShapeDtypeStruct((ROWS, WIDTH), BF16),
            jax.ShapeDtypeStruct((16, Q * BLK), F32),
            jax.ShapeDtypeStruct((16, Q * BLK), F32),
        ),
        in_specs=[VM] * 8,
        out_specs=(VM,) * 3,
        scratch_shapes=[
            pltpu.VMEM((Y, ROWS, WIDTH), BF16),
            pltpu.VMEM((Y, ROWS, WIDTH), BF16),
            pltpu.VMEM((2, ROWS, WIDTH), BF16),
            pltpu.VMEM((2, 2, ROWS, WIDTH), BF16),
            pltpu.VMEM((KB, 2, 3) + tile, BF16),
            pltpu.VMEM((KB, 2, 4) + tile, BF16),
            pltpu.VMEM((KB,) + tile, BF16),
            pltpu.VMEM((2,) + tile, BF16),
            pltpu.VMEM((2, 2) + tile, BF16),
            pltpu.VMEM((Z, 2) + tile, BF16),
            pltpu.VMEM((Z, 2, 2) + tile, BF16),
            pltpu.VMEM((Z,) + tile, BF16),
            pltpu.VMEM((2, 3) + tile, BF16),
            pltpu.VMEM((2, 4) + tile, BF16),
            pltpu.VMEM((2,) + tile, BF16),
            pltpu.VMEM((2, Q, 16, BLK), BF16),
            pltpu.SemaphoreType.DMA((112,)),
            pltpu.SemaphoreType.DMA((112,)),
        ],
        compiler_params=pltpu.CompilerParams(collective_id=2, has_side_effects=True),
    )(back, din, dout, x, up, coeff, readout, gain)


def on_device(
    inputs, norm_gain, w_in, w_out, block_index, segment_ids, teacher_scores, upstream, readout
):
    scale = 1.0 / math.sqrt(ROWS * X * Q * Z)
    gain, head, teacher = norm_gain[None, :], readout[None, :], teacher_scores[None, :]
    table = jnp.pad(block_index, ((0, 0), (0, BLK - KB)))
    seg = jnp.pad(segment_ids.astype(F32), (0, BLK - ROWS), constant_values=-1.0)
    seg = jnp.broadcast_to(seg[None, :], (8, BLK))
    nrm_all, up_all, win_all, wout_all, bi_all = gather_all(inputs, upstream, gain, w_in, w_out, table)
    nrm = nrm_all.reshape(Q * ROWS, WIDTH)
    part, act, slope = forward(bi_all, nrm, win_all, wout_all)
    layer_out, coeff = branch_sum(part.reshape(Q, ROWS, WIDTH), inputs, seg, teacher, head)
    back, din, dout = backward(
        bi_all, up_all.reshape(Q * ROWS, WIDTH), coeff, head, nrm, win_all, wout_all, act, slope)
    input_grad, grad_in, grad_out = finish(
        scale, back.reshape(Q, ROWS, WIDTH), din, dout, inputs, upstream, coeff, head, gain)
    return layer_out, input_grad, grad_in, grad_out


def solution(mesh):
    return jax.shard_map(
        on_device,
        mesh=mesh,
        in_specs=(
            P(("tok", "feat"), None),
            P(),
            P("tok", "feat"),
            P("tok", "feat"),
            P("feat", None),
            P(("tok", "feat")),
            P(),
            P(("tok", "feat"), None),
            P(),
        ),
        out_specs=(
            P(("tok", "feat"), None),
            P(("tok", "feat"), None),
            P("tok", "feat"),
            P("tok", "feat"),
        ),
        check_vma=False,
    )
```

```python
import functools
import heapq
import math

import jax
import jax.numpy as jnp
from jax import lax
from jax.experimental import pallas as pl
from jax.experimental.pallas import tpu as pltpu
from jax.sharding import PartitionSpec as P

BLK = 128
EPS = 1e-06
LOSS_WEIGHT = 8.0
X, Y, C, Z = 4, 4, 2, 8
Q = Y * C
ROWS = 64
WIDTH = 2048
KB = 4
MESH = pl.DeviceIdType.MESH
F32, BF16 = jnp.float32, jnp.bfloat16
NT = (((1,), (1,)), ((), ()))
NN = (((1,), (0,)), ((), ()))
VM = pl.BlockSpec(memory_space=pltpu.VMEM)
ANY = pl.BlockSpec(memory_space=pl.ANY)


def dot(a, b, dims):
    return lax.dot_general(a, b, dims, preferred_element_type=F32)


class Place:
    def __init__(self):
        t = lax.axis_index("tok")
        self.z = lax.axis_index("feat")
        self.t = t
        self.q = lax.rem(t, Q)
        self.c = lax.rem(t, C)
        self.y = lax.rem(t // C, Y)
        self.x = t // Q

    def at(self, x=None, y=None, c=None, z=None):
        x, y = self.x if x is None else x, self.y if y is None else y
        c, z = self.c if c is None else c, self.z if z is None else z
        return {"tok": (x * Y + y) * C + c, "feat": z}

    def sibling(self):
        return self.at(c=1 - self.c)

    def along(self, axis, by):
        n = {"x": X, "y": Y, "z": Z}[axis]
        me = {"x": self.x, "y": self.y, "z": self.z}[axis]
        return self.at(**{axis: lax.rem(me + by + n, n)})

    def member(self, by):
        return {"tok": self.x * Q + lax.rem(self.q + by + Q, Q), "feat": self.z}

    def plane(self, dx, by):
        return {"tok": lax.rem(self.x + dx + X, X) * Q + lax.rem(self.q + by + Q, Q), "feat": self.z}

    def flat(self, by):
        n = X * Q * Z
        d = lax.rem(self.t * Z + self.z + by + n, n)
        return {"tok": d // Z, "feat": lax.rem(d, Z)}


class Mail:
    def __init__(self, send_sem, recv_sem):
        self.send_sem, self.recv_sem, self.sent = send_sem, recv_sem, []

    def send(self, src, dst, to):
        i = len(self.sent)
        copy = pltpu.make_async_remote_copy(
            src_ref=src,
            dst_ref=dst,
            send_sem=self.send_sem.at[i],
            recv_sem=self.recv_sem.at[i],
            device_id=to,
            device_id_type=MESH,
        )
        copy.start()
        self.sent.append(copy)
        return copy

    def close(self):
        for copy in self.sent:
            copy.wait_send()


def greet(devices, meanwhile=None):
    barrier = pltpu.get_barrier_semaphore()
    for device in devices:
        pl.semaphore_signal(barrier, inc=1, device_id=device, device_id_type=MESH)
    if meanwhile:
        meanwhile()
    pl.semaphore_wait(barrier, len(devices))


class Flows:
    def __init__(self):
        self.heap, self.now, self.count = [], 0.0, 0

    def add(self, flow):
        heapq.heappush(self.heap, (self.now, self.count, flow))
        self.count += 1

    def run(self):
        while self.heap:
            self.now, _, flow = heapq.heappop(self.heap)
            for delay in flow:
                heapq.heappush(self.heap, (self.now + delay, self.count, flow))
                self.count += 1
                break


def gather_ring(mail, n, me, plus, minus, piece, half, delays, arrived=None):
    a = mail.send(piece(me), piece(me), plus)
    b = mail.send(piece(me), piece(me), minus)
    for step in range(1, n // 2 + 1):
        yield delays[step - 1]
        last = step == n // 2
        a.wait_recv()
        left = lax.rem(me - step + n, n)
        if not last:
            ref = half(left, 0) if step == n // 2 - 1 else piece(left)
            a = mail.send(ref, ref, plus)
            if arrived:
                arrived(left, None)
        elif arrived:
            arrived(left, 0)
        b.wait_recv()
        right = lax.rem(me + step, n)
        if not last:
            ref = half(right, 1) if step == n // 2 - 1 else piece(right)
            b = mail.send(ref, ref, minus)
            if arrived:
                arrived(right, None)
        elif arrived:
            arrived(right, 1)


def reduce_ring(mail, n, plus, minus, own, half, stage, land, delays, done):
    steps = n // 2
    a = mail.send(half(own(steps), 0), half(land(0, 1), 0), plus)
    b = mail.send(half(own(steps), 1), half(land(1, 1), 1), minus)
    for step in range(2, steps + 1):
        yield delays[step - 2]
        for way in (0, 1):
            mine = own(steps - step + 1 if way == 0 else n - steps + step - 1)
            (a, b)[way].wait_recv()
            came, out = land(way, step - 1), stage(way, step)
            if step == 2:
                half(out, way)[...] = (half(mine, way)[...].astype(F32) + half(came, way)[...].astype(F32)).astype(BF16)
                half(out, 1 - way)[...] = half(mine, 1 - way)[...]
            else:
                out[...] = (mine[...].astype(F32) + came[...].astype(F32)).astype(BF16)
            sent = mail.send(out, land(way, step), minus if way else plus)
            if way == 0:
                a = sent
            else:
                b = sent
    yield delays[steps - 1]
    mine = own(0)
    a.wait_recv()
    b.wait_recv()
    done(mine[...].astype(F32) + land(0, steps)[...].astype(F32) + land(1, steps)[...].astype(F32))


def gather_kernel(x_ref, up_ref, gain_ref, win_ref, wout_ref, bi_ref,
                  nrm_all, up_all, win_all, wout_all, bi_all,
                  x_v, gain_v, nrm_v, send_sem, recv_sem, local_sem):
    p = Place()
    mail = Mail(send_sem, recv_sem)
    local = []

    def keep(src, dst):
        copy = pltpu.make_async_copy(src, dst, local_sem.at[len(local)])
        copy.start()
        local.append(copy)
        return copy

    loads = [keep(x_ref, x_v), keep(gain_ref, gain_v)]
    greet([p.plane(dx, o) for dx in range(X) for o in range(Q) if dx or o] + [p.along("z", s) for s in (-1, 1)])
    flows = Flows()
    yplus, yminus = p.along("y", 1), p.along("y", -1)
    zplus, zminus = p.along("z", 1), p.along("z", -1)

    def columns(ref, q):
        return ref.at[:, pl.ds(pl.multiple_of(q * BLK, BLK), BLK)]

    def my_rows(ref):
        return ref.at[pl.ds(pl.multiple_of(p.q * 16, 16), 16), :]

    in_slab, out_slab = win_all.at[p.z, p.x], wout_all.at[p.x, p.z]
    in_deals, out_deals = {}, []
    for o in range(Q):
        q = lax.rem(p.q + o, Q)
        for dx in range(X):
            if dx or o:
                in_deals[dx, o] = mail.send(columns(win_ref, q), my_rows(in_slab), p.plane(dx, o))
        if o:
            out_deals.append(mail.send(columns(wout_ref, q), my_rows(out_slab), p.member(o)))
    slab_copies = [keep(columns(win_ref, p.q), my_rows(in_slab)), keep(columns(wout_ref, p.q), my_rows(out_slab))]

    def tokens(own, out, first):
        def half(y, h):
            return out.at[y * C + p.c, pl.ds(h * 32, 32), :]

        def mine(h):
            return own.at[pl.ds(h * 32, 32), :]

        relays = []

        def pass_on(ref, to):
            relays.append(mail.send(ref, ref, to))
            return relays[-1]

        a0 = mail.send(mine(0), half(p.y, 0), yplus)
        b1 = mail.send(mine(1), half(p.y, 1), yminus)
        a1 = mail.send(mine(1), half(p.y, 1), yplus)
        b0 = mail.send(mine(0), half(p.y, 0), yminus)
        relays.append(mail.send(own, out.at[p.q], p.sibling()))
        keep(own, out.at[p.q])
        left, right, far = lax.rem(p.y + 3, Y), lax.rem(p.y + 1, Y), lax.rem(p.y + 2, Y)
        yield first
        a0.wait_recv()
        fa = mail.send(half(left, 0), half(left, 0), yplus)
        pass_on(half(left, 0), p.sibling())
        b1.wait_recv()
        fb = mail.send(half(right, 1), half(right, 1), yminus)
        pass_on(half(right, 1), p.sibling())
        yield 3.0
        a1.wait_recv()
        pass_on(half(left, 1), p.sibling())
        b0.wait_recv()
        pass_on(half(right, 0), p.sibling())
        yield 8.3
        fa.wait_recv()
        pass_on(half(far, 0), p.sibling())
        fb.wait_recv()
        pass_on(half(far, 1), p.sibling())
        yield 2.0
        for copy in relays:
            copy.wait_recv()

    def table():
        mine = bi_all.at[p.z]
        keep(bi_ref, mine)
        a = mail.send(bi_ref, mine, zplus)
        b = mail.send(bi_ref, mine, zminus)
        for step in range(1, Z // 2 + 1):
            yield 2.5
            a.wait_recv()
            left = bi_all.at[lax.rem(p.z - step + Z, Z)]
            if step < Z // 2:
                a = mail.send(left, left, zplus)
                b.wait_recv()
                right = bi_all.at[lax.rem(p.z + step, Z)]
                if step < Z // 2 - 1:
                    b = mail.send(right, right, zminus)

    flows.add(tokens(up_ref, up_all, 4.5))
    flows.add(table())
    quick = [2.5] * 4

    def w_in_z(k):
        return gather_ring(
            mail, Z, p.z, zplus, zminus,
            lambda z: win_all.at[z, k],
            lambda z, h: win_all.at[z, k, pl.ds(h * 64, 64), :],
            [3.0] * 4)

    def w_out_x(z):
        ref = wout_all.at[p.x, z]
        copies = [mail.send(ref, ref, p.along("x", dx)) for dx in (1, 2, 3)]
        yield 6.0
        for copy in copies:
            copy.wait_recv()

    def w_in():
        yield 2.5
        slab_copies[0].wait()
        for dx in range(X):
            for o in range(Q):
                if dx or o:
                    in_deals[dx, o].wait_recv()
            flows.add(w_in_z(lax.rem(p.x - dx + X, X)))
            yield 0.3

    def w_out():
        yield 2.6
        slab_copies[1].wait()
        for copy in out_deals:
            copy.wait_recv()
        seen = []

        def got(z, h):
            if h is not None:
                seen.append(h)
            if h is None or len(seen) == 2:
                flows.add(w_out_x(z))

        flows.add(gather_ring(
            mail, Z, p.z, zplus, zminus,
            lambda z: wout_all.at[p.x, z],
            lambda z, h: wout_all.at[p.x, z, pl.ds(h * 64, 64), :],
            quick, got))
        flows.add(w_out_x(p.z))

    flows.add(w_in())
    flows.add(w_out())

    def normed():
        for copy in loads:
            copy.wait()
        xf = x_v[...].astype(F32)
        inv = lax.rsqrt(jnp.mean(xf * xf, axis=1, keepdims=True) + EPS)
        nrm_v[...] = (xf * inv * gain_v[...]).astype(BF16)
        yield from tokens(nrm_v, nrm_all, 10.0)

    flows.add(normed())
    flows.run()
    for copy in local[4:]:
        copy.wait()
    mail.close()


def gather_all(x, up, gain, w_in, w_out, table):
    far = pl.BlockSpec(memory_space=pltpu.HBM)
    return pl.pallas_call(
        gather_kernel,
        name="gather_all",
        out_shape=(
            jax.ShapeDtypeStruct((Q, ROWS, WIDTH), BF16),
            jax.ShapeDtypeStruct((Q, ROWS, WIDTH), BF16),
            jax.ShapeDtypeStruct((Z, KB, BLK, BLK), BF16),
            jax.ShapeDtypeStruct((KB, Z, BLK, BLK), BF16),
            jax.ShapeDtypeStruct((Z, KB, Z), jnp.int32),
        ),
        in_specs=[far] * 6,
        out_specs=(ANY,) * 5,
        scratch_shapes=[
            pltpu.VMEM((ROWS, WIDTH), BF16),
            pltpu.VMEM((1, WIDTH), F32),
            pltpu.VMEM((ROWS, WIDTH), BF16),
            pltpu.SemaphoreType.DMA((136,)),
            pltpu.SemaphoreType.DMA((136,)),
            pltpu.SemaphoreType.DMA((8,)),
        ],
        compiler_params=pltpu.CompilerParams(collective_id=0, has_side_effects=True, vmem_limit_bytes=4 << 20),
    )(x, up, gain, w_in, w_out, table)


SQ = math.sqrt(2.0 / math.pi)
UNROLL = 8


def forward_kernel(bi_ref, nrm_ref, win_ref, wout_ref, part_ref, act_ref, slope_ref, wide_ref, blocks_ref, acc):
    q = lax.rem(lax.axis_index("tok"), Q)
    acc[...] = jnp.zeros_like(acc)
    wide_ref[...] = jnp.zeros_like(wide_ref)
    for d in range(WIDTH // BLK):
        blocks_ref[d] = nrm_ref[:, d * BLK:(d + 1) * BLK]

    def block(j, carry):
        at = [pl.multiple_of(bi_ref[j, k, q] * BLK, BLK) for k in range(KB)]
        for k in range(KB):
            wide_ref[pl.ds(at[k], BLK), pl.ds(pl.multiple_of(j * BLK, BLK), BLK)] = win_ref[j, k]
        picked = jnp.concatenate([nrm_ref[:, pl.ds(a, BLK)] for a in at], axis=1)
        v = dot(picked, win_ref[j].reshape(KB * BLK, BLK), NN)
        tanh = jnp.tanh(SQ * (v + 0.044715 * (v * v * v)))
        act = 0.5 * v * (1.0 + tanh)
        slope = 0.5 * (1.0 + tanh) + 0.5 * v * (1.0 - tanh * tanh) * (SQ * (1.0 + 3.0 * 0.044715 * (v * v)))
        act_half = act.astype(BF16)
        act_ref[j] = act.T.astype(BF16)
        slope_ref[j] = slope
        w_out = jnp.concatenate([wout_ref[k, j] for k in range(KB)], axis=0)
        terms = dot(act_half, w_out, NT)
        for k in range(KB):
            acc[:, pl.ds(at[k], BLK)] += terms[:, k * BLK:(k + 1) * BLK]
        return carry

    lax.fori_loop(0, Z, block, 0, unroll=UNROLL)
    part_ref[...] = acc[...].astype(BF16)


def forward(table, nrm, w_in, w_out):
    n = Q * ROWS
    return pl.pallas_call(
        forward_kernel,
        name="forward",
        out_shape=(
            jax.ShapeDtypeStruct((n, WIDTH), BF16),
            jax.ShapeDtypeStruct((Z, BLK, n), BF16),
            jax.ShapeDtypeStruct((Z, n, BLK), F32),
            jax.ShapeDtypeStruct((WIDTH, Z * BLK), BF16),
            jax.ShapeDtypeStruct((WIDTH // BLK, n, BLK), BF16),
        ),
        in_specs=[pl.BlockSpec(memory_space=pltpu.SMEM), VM, VM, VM],
        out_specs=(VM,) * 5,
        scratch_shapes=[pltpu.VMEM((n, WIDTH), F32)],
        compiler_params=pltpu.CompilerParams(vmem_limit_bytes=20<<20),
    )(table, nrm, w_in, w_out)


def halves(ref, h):
    return ref.at[pl.ds(h * 32, 32), :]


def reduce_tokens(mail, p, part, rs, pair, stage, land, done, times):
    other = 1 - p.c
    sends = {}
    ys = [lax.rem(p.y + o, Y) for o in range(Y)]
    for o in (2, 1, 3, 0):
        sends[o] = mail.send(part(ys[o] * C + other), rs.at[ys[o]], p.sibling())
    plus, minus = p.along("y", 1), p.along("y", -1)
    yield times[0]

    def fold(o):
        sends[o].wait_recv()
        pair[ys[o]] = (part(ys[o] * C + p.c)[...].astype(F32) + rs[ys[o]].astype(F32)).astype(BF16)

    fold(2)
    a = mail.send(halves(pair.at[ys[2]], 0), land.at[0, 0], plus)
    b = mail.send(halves(pair.at[ys[2]], 1), land.at[1, 0], minus)
    fold(1)
    a1 = mail.send(halves(pair.at[ys[1]], 1), land.at[0, 1], plus)
    fold(3)
    b1 = mail.send(halves(pair.at[ys[3]], 0), land.at[1, 1], minus)
    fold(0)
    yield times[1]
    a.wait_recv()
    stage[0] = (pair[ys[1], 0:32].astype(F32) + land[0, 0].astype(F32)).astype(BF16)
    a2 = mail.send(stage.at[0], land.at[0, 2], plus)
    b.wait_recv()
    stage[1] = (pair[ys[3], 32:64].astype(F32) + land[1, 0].astype(F32)).astype(BF16)
    b2 = mail.send(stage.at[1], land.at[1, 2], minus)
    yield times[2]
    for copy in (a1, b1, a2, b2):
        copy.wait_recv()
    top = pair[ys[0], 0:32].astype(F32) + land[0, 2].astype(F32) + land[1, 1].astype(F32)
    low = pair[ys[0], 32:64].astype(F32) + land[0, 1].astype(F32) + land[1, 2].astype(F32)
    done(jnp.concatenate([top, low], axis=0))


def branch_kernel(part_ref, x_ref, seg_ref, teacher_ref, readout_ref,
                  lo_ref, coeff_ref,
                  rs, pair, stage, land, ids, scores, send_sem, recv_sem):
    p = Place()
    mail = Mail(send_sem, recv_sem)
    near = [p.flat(1), p.flat(-1)]
    greet([p.member(o) for o in range(1, Q)] + near)
    ids[0] = jnp.full((8, BLK), -1.0, F32)
    ids[0, 0:1, 0:ROWS] = seg_ref[...].astype(F32)
    id_copies = [mail.send(ids.at[0], ids.at[1 + i], near[i]) for i in (0, 1)]
    total = []
    flows = Flows()
    flows.add(reduce_tokens(mail, p, lambda q: part_ref.at[q], rs, pair, stage, land, total.append, [1.0, 4.0, 4.0]))
    eye = lax.broadcasted_iota(jnp.int32, (ROWS, BLK), 0) == lax.broadcasted_iota(jnp.int32, (ROWS, BLK), 1)
    ids_col = jnp.sum(jnp.where(eye, ids[0, 0:1, :], 0.0), axis=1, keepdims=True)
    segs = teacher_ref.shape[1]
    hot = lax.broadcasted_iota(jnp.int32, (ROWS, segs), 1).astype(F32) == ids_col
    teacher = jnp.sum(jnp.where(hot, teacher_ref[...], 0.0), axis=1, keepdims=True)
    flows.run()
    lo = (x_ref[...].astype(F32) + total[0]).astype(BF16)
    lo_ref[...] = lo
    score = jnp.sum(lo.astype(F32) * readout_ref[...], axis=1, keepdims=True)
    score_row = jnp.sum(jnp.where(eye, score, 0.0), axis=0, keepdims=True)
    scores[0] = jnp.broadcast_to(score_row, (8, BLK))
    copies = [mail.send(scores.at[0], scores.at[1 + i], near[i]) for i in (0, 1)]
    for copy in id_copies + copies:
        copy.wait_recv()
    sums = jnp.zeros((ROWS, 1), F32)
    counts = jnp.zeros((ROWS, 1), F32)
    for i in range(3):
        same = ids[i, 0:1, :] == ids_col
        sums += jnp.sum(jnp.where(same, scores[i, 0:1, :], 0.0), axis=1, keepdims=True)
        counts += jnp.sum(jnp.where(same, 1.0, 0.0), axis=1, keepdims=True)
    coeff = (2.0 * LOSS_WEIGHT) * (sums / counts - teacher)
    coeff_row = jnp.sum(jnp.where(eye, coeff, 0.0), axis=0, keepdims=True)
    coeff_ref[p.q] = jnp.broadcast_to(coeff_row, (8, BLK))
    out = [mail.send(coeff_ref.at[p.q], coeff_ref.at[p.q], p.member(o)) for o in range(1, Q)]
    for copy in out:
        copy.wait_recv()
    mail.close()


def branch_sum(part, x, seg, teacher, readout):
    return pl.pallas_call(
        branch_kernel,
        name="branch_sum",
        out_shape=(
            jax.ShapeDtypeStruct((ROWS, WIDTH), BF16),
            jax.ShapeDtypeStruct((Q, 8, BLK), F32),
        ),
        in_specs=[VM] * 5,
        out_specs=(VM,) * 2,
        scratch_shapes=[
            pltpu.VMEM((Y, ROWS, WIDTH), BF16),
            pltpu.VMEM((Y, ROWS, WIDTH), BF16),
            pltpu.VMEM((2, ROWS // 2, WIDTH), BF16),
            pltpu.VMEM((2, 3, ROWS // 2, WIDTH), BF16),
            pltpu.VMEM((3, 8, BLK), F32),
            pltpu.VMEM((3, 8, BLK), F32),
            pltpu.SemaphoreType.DMA((32,)),
            pltpu.SemaphoreType.DMA((32,)),
        ],
        compiler_params=pltpu.CompilerParams(collective_id=1, has_side_effects=True, vmem_limit_bytes=12<<20),
    )(part, x, seg, teacher, readout)


def rows64(ref, h):
    return ref.at[pl.ds(h * 64, 64), :]


FAR_FIRST = (4, 3, 5, 2, 6, 1, 7, 0)


def backward_kernel(scale, bi_ref, up_all, coeff_ref, readout_ref, nrm_ref, wout_ref, act_ref, slope_ref, wide_ref,
                    x_ref, up_ref, gain_ref,
                    ig_ref, gin_ref, gout_ref,
                    cot, pre, back, din, dout,
                    rs, pair, stage, land,
                    za_stage, za_land, za_sum,
                    xb_land, xb_sum, zb_stage, zb_land,
                    slab, dealt_in, dealt, send_sem, recv_sem):
    p = Place()
    mail = Mail(send_sem, recv_sem)
    eye = lax.broadcasted_iota(jnp.int32, (ROWS, BLK), 0) == lax.broadcasted_iota(jnp.int32, (ROWS, BLK), 1)

    def form():
        for b in range(Q):
            rows = slice(b * ROWS, (b + 1) * ROWS)
            coeff = jnp.sum(jnp.where(eye, coeff_ref[b, 0:1, :], 0.0), axis=1, keepdims=True)
            value = (up_all[rows, :].astype(F32) + coeff * readout_ref[...]).astype(BF16)
            for d in range(WIDTH // BLK):
                cot[d, rows, :] = value[:, d * BLK:(d + 1) * BLK]

    def block(dz):
        j = lax.rem(p.z + dz, Z)
        at = [bi_ref[j, k, p.q] for k in range(KB)]
        picked = jnp.concatenate([cot[a] for a in at], axis=1)
        chosen = jnp.concatenate([nrm_ref[a] for a in at], axis=1)
        w_out = jnp.concatenate([wout_ref[k, j] for k in range(KB)], axis=0)
        value = dot(picked, w_out, NN) * slope_ref[j]
        pre[:, pl.ds(pl.multiple_of(j * BLK, BLK), BLK)] = value.astype(BF16)
        d_in = (dot(value.T.astype(BF16), chosen, NN) * scale).astype(BF16)
        d_out = (dot(act_ref[j], picked, NN) * scale).astype(BF16)
        for k in range(KB):
            cols = slice(k * BLK, (k + 1) * BLK)
            din[dz, k] = d_in[:, cols]
            dout[dz, k] = d_out[:, cols]

    def first():
        form()
        block(FAR_FIRST[0])

    greet([p.plane(dx, o) for dx in range(X) for o in range(Q) if dx or o] + [p.along("z", s) for s in (-1, 1)], first)
    zplus, zminus = p.along("z", 1), p.along("z", -1)
    flows = Flows()
    ready = {FAR_FIRST[0]}
    total, deals, x_sends = [], [], {}

    def out_x(dz):
        for dx in (1, 2, 3):
            x = lax.rem(p.x + dx, X)
            x_sends[dz, dx] = mail.send(dout.at[dz, x], xb_land.at[dx - 1, dz], p.along("x", dx))

    def in_z(dx):
        k = lax.rem(p.x + dx, X)

        def own(dz):
            assert dz in ready
            return din.at[dz, k]

        def done(value):
            za_sum[dx] = value.T.astype(BF16)
            for o in range(Q):
                rows = pl.ds(pl.multiple_of(lax.rem(p.q + o, Q) * 16, 16), 16)
                if dx == 0 and o == 0:
                    dealt_in[p.x, p.q] = za_sum[dx, rows, :]
                else:
                    deals.append(mail.send(za_sum.at[dx, rows, :], dealt_in.at[p.x, p.q], p.plane(dx, o)))

        return reduce_ring(
            mail, Z, zplus, zminus, own, rows64,
            lambda way, step: za_stage.at[dx, way, step - 2], lambda way, step: za_land.at[dx, way, step - 1],
            [3.2] * 4, done)

    summed = set()

    def out_own(dz):
        if dz not in summed:
            assert dz in ready
            summed.add(dz)
            for dx in (1, 2, 3):
                x_sends[dz, dx].wait_recv()
            value = dout[dz, p.x].astype(F32) + sum(xb_land[i, dz].astype(F32) for i in range(3))
            xb_sum[dz] = value.astype(BF16)
        return xb_sum.at[dz]

    def deal(value):
        slab[...] = value.T.astype(BF16)
        dealt[p.q] = slab[pl.ds(pl.multiple_of(p.q * 16, 16), 16), :]
        for o in range(1, Q):
            rows = slab.at[pl.ds(pl.multiple_of(lax.rem(p.q + o, Q) * 16, 16), 16), :]
            deals.append(mail.send(rows, dealt.at[p.q], p.member(o)))

    def out_z():
        yield 3.5
        yield from reduce_ring(
            mail, Z, zplus, zminus, out_own, rows64,
            lambda way, step: zb_stage.at[way, step - 2], lambda way, step: zb_land.at[way, step - 1],
            [3.0, 3.0, 3.0, 3.0], deal)

    def compute():
        out_x(FAR_FIRST[0])
        for dz in FAR_FIRST[1:]:
            block(dz)
            ready.add(dz)
            out_x(dz)
            yield 1.0
        for n in range(4):
            cols = slice(n * 512, (n + 1) * 512)
            back[:, cols] = dot(pre[...], wide_ref[cols, :], NT).astype(BF16)
        flows.add(reduce_tokens(
            mail, p, lambda q: back.at[pl.ds(pl.multiple_of(q * ROWS, ROWS), ROWS), :],
            rs, pair, stage, land, total.append, [1.0, 5.0, 6.0]))

    for dx in (1, 2, 3, 0):
        flows.add(in_z(dx))
    flows.add(compute())
    flows.add(out_z())
    flows.run()

    xf = x_ref[...].astype(F32)
    inv = lax.rsqrt(jnp.mean(xf * xf, axis=1, keepdims=True) + EPS)
    coeff = jnp.sum(jnp.where(eye, coeff_ref[p.q][0:1, :], 0.0), axis=1, keepdims=True)
    own_cot = (up_ref[...].astype(F32) + coeff * readout_ref[...]).astype(BF16).astype(F32)
    scaled = total[0] * gain_ref[...]
    inner = jnp.mean(scaled * xf, axis=1, keepdims=True)
    ig_ref[...] = (own_cot + (inv * scaled - xf * (inv * inv * inv) * inner)).astype(BF16)
    for copy in deals:
        copy.wait_recv()
    for q in range(Q):
        cols = slice(q * BLK, (q + 1) * BLK)
        gin_ref[:, cols] = sum(dealt_in[x, q].astype(F32) for x in range(X))
        gout_ref[:, cols] = dealt[q].astype(F32)
    mail.close()


def backward(scale, table, up_all, coeff, readout, nrm, w_out, act, slope, wide, x, up, gain):
    n = Q * ROWS
    tile = (BLK, BLK)
    return pl.pallas_call(
        functools.partial(backward_kernel, scale),
        name="backward",
        out_shape=(
            jax.ShapeDtypeStruct((ROWS, WIDTH), BF16),
            jax.ShapeDtypeStruct((16, Q * BLK), F32),
            jax.ShapeDtypeStruct((16, Q * BLK), F32),
        ),
        in_specs=[pl.BlockSpec(memory_space=pltpu.SMEM)] + [VM] * 11,
        out_specs=(VM,) * 3,
        scratch_shapes=[
            pltpu.VMEM((WIDTH // BLK, n, BLK), BF16),
            pltpu.VMEM((n, Z * BLK), BF16),
            pltpu.VMEM((n, WIDTH), BF16),
            pltpu.VMEM((Z, KB) + tile, BF16),
            pltpu.VMEM((Z, KB) + tile, BF16),
            pltpu.VMEM((Y, ROWS, WIDTH), BF16),
            pltpu.VMEM((Y, ROWS, WIDTH), BF16),
            pltpu.VMEM((2, ROWS // 2, WIDTH), BF16),
            pltpu.VMEM((2, 3, ROWS // 2, WIDTH), BF16),
            pltpu.VMEM((KB, 2, 3) + tile, BF16),
            pltpu.VMEM((KB, 2, 4) + tile, BF16),
            pltpu.VMEM((KB,) + tile, BF16),
            pltpu.VMEM((3, Z) + tile, BF16),
            pltpu.VMEM((Z,) + tile, BF16),
            pltpu.VMEM((2, 3) + tile, BF16),
            pltpu.VMEM((2, 4) + tile, BF16),
            pltpu.VMEM(tile, BF16),
            pltpu.VMEM((X, Q, 16, BLK), BF16),
            pltpu.VMEM((Q, 16, BLK), BF16),
            pltpu.SemaphoreType.DMA((128,)),
            pltpu.SemaphoreType.DMA((128,)),
        ],
        compiler_params=pltpu.CompilerParams(collective_id=2, has_side_effects=True, vmem_limit_bytes=36 << 20),
    )(table, up_all, coeff, readout, nrm, w_out, act, slope, wide, x, up, gain)


def on_device(
    inputs, norm_gain, w_in, w_out, block_index, segment_ids, teacher_scores, upstream, readout
):
    scale = 1.0 / math.sqrt(ROWS * X * Q * Z)
    gain, head, teacher = norm_gain[None, :], readout[None, :], teacher_scores[None, :]
    table = block_index.T
    seg = segment_ids[None, :]
    nrm_all, up_all, win_all, wout_all, bi_all = gather_all(
        *[pltpu.with_memory_space_constraint(a, pltpu.HBM) for a in (inputs, upstream, gain, w_in, w_out, table)])
    nrm = nrm_all.reshape(Q * ROWS, WIDTH)
    part, act, slope, wide, blocks = forward(bi_all, nrm, win_all, wout_all)
    layer_out, coeff = branch_sum(part.reshape(Q, ROWS, WIDTH), inputs, seg, teacher, head)
    input_grad, grad_in, grad_out = backward(
        scale, bi_all, up_all.reshape(Q * ROWS, WIDTH), coeff, head, blocks, wout_all, act, slope, wide,
        inputs, upstream, gain)
    return layer_out, input_grad, grad_in, grad_out


def solution(mesh):
    return jax.shard_map(
        on_device,
        mesh=mesh,
        in_specs=(
            P(("tok", "feat"), None),
            P(),
            P("tok", "feat"),
            P("tok", "feat"),
            P("feat", None),
            P(("tok", "feat")),
            P(),
            P(("tok", "feat"), None),
            P(),
        ),
        out_specs=(
            P(("tok", "feat"), None),
            P(("tok", "feat"), None),
            P("tok", "feat"),
            P("tok", "feat"),
        ),
        check_vma=False,
    )
```

```python
import functools
import heapq
import math

import jax
import jax.numpy as jnp
from jax import lax
from jax.experimental import pallas as pl
from jax.experimental.pallas import tpu as pltpu
from jax.sharding import PartitionSpec as P

BLK = 128
EPS = 1e-06
LOSS_WEIGHT = 8.0
X, Y, C, Z = 4, 4, 2, 8
Q = Y * C
ROWS = 64
WIDTH = 2048
KB = 4
MESH = pl.DeviceIdType.MESH
F32, BF16 = jnp.float32, jnp.bfloat16
NT = (((1,), (1,)), ((), ()))
NN = (((1,), (0,)), ((), ()))
VM = pl.BlockSpec(memory_space=pltpu.VMEM)
ANY = pl.BlockSpec(memory_space=pl.ANY)


def dot(a, b, dims):
    return lax.dot_general(a, b, dims, preferred_element_type=F32)


class Place:
    def __init__(self):
        t = lax.axis_index("tok")
        self.z = lax.axis_index("feat")
        self.t = t
        self.q = lax.rem(t, Q)
        self.c = lax.rem(t, C)
        self.y = lax.rem(t // C, Y)
        self.x = t // Q

    def at(self, x=None, y=None, c=None, z=None):
        x, y = self.x if x is None else x, self.y if y is None else y
        c, z = self.c if c is None else c, self.z if z is None else z
        return {"tok": (x * Y + y) * C + c, "feat": z}

    def sibling(self):
        return self.at(c=1 - self.c)

    def along(self, axis, by):
        n = {"x": X, "y": Y, "z": Z}[axis]
        me = {"x": self.x, "y": self.y, "z": self.z}[axis]
        return self.at(**{axis: lax.rem(me + by + n, n)})

    def member(self, by):
        return {"tok": self.x * Q + lax.rem(self.q + by + Q, Q), "feat": self.z}

    def plane(self, dx, by):
        return {"tok": lax.rem(self.x + dx + X, X) * Q + lax.rem(self.q + by + Q, Q), "feat": self.z}

    def flat(self, by):
        n = X * Q * Z
        d = lax.rem(self.t * Z + self.z + by + n, n)
        return {"tok": d // Z, "feat": lax.rem(d, Z)}


class Mail:
    def __init__(self, send_sem, recv_sem):
        self.send_sem, self.recv_sem, self.sent = send_sem, recv_sem, []

    def send(self, src, dst, to):
        i = len(self.sent)
        copy = pltpu.make_async_remote_copy(
            src_ref=src,
            dst_ref=dst,
            send_sem=self.send_sem.at[i],
            recv_sem=self.recv_sem.at[i],
            device_id=to,
            device_id_type=MESH,
        )
        copy.start()
        self.sent.append(copy)
        return copy

    def close(self):
        for copy in self.sent:
            copy.wait_send()


def greet(devices, meanwhile=None):
    barrier = pltpu.get_barrier_semaphore()
    for device in devices:
        pl.semaphore_signal(barrier, inc=1, device_id=device, device_id_type=MESH)
    if meanwhile:
        meanwhile()
    pl.semaphore_wait(barrier, len(devices))


class Flows:
    def __init__(self):
        self.heap, self.now, self.count = [], 0.0, 0
        self.ended, self.pending = set(), []

    def add(self, flow, name=None):
        heapq.heappush(self.heap, (self.now, self.count, flow, name))
        self.count += 1

    def after(self, names, start):
        self.pending.append((set(names), start))

    def end(self, name):
        self.ended.add(name)
        for names, start in list(self.pending):
            if names <= self.ended:
                self.pending.remove((names, start))
                start()

    def run(self):
        while self.heap:
            self.now, _, flow, name = heapq.heappop(self.heap)
            for delay in flow:
                heapq.heappush(self.heap, (self.now + delay, self.count, flow, name))
                self.count += 1
                break
            else:
                if name is not None:
                    self.end(name)
        assert not self.pending


def gather_ring(mail, n, me, plus, minus, piece, half, delays, arrived=None):
    a = mail.send(piece(me), piece(me), plus)
    b = mail.send(piece(me), piece(me), minus)
    for step in range(1, n // 2 + 1):
        yield delays[step - 1]
        last = step == n // 2
        a.wait_recv()
        left = lax.rem(me - step + n, n)
        if not last:
            ref = half(left, 0) if step == n // 2 - 1 else piece(left)
            a = mail.send(ref, ref, plus)
            if arrived:
                arrived(left, None)
        elif arrived:
            arrived(left, 0)
        b.wait_recv()
        right = lax.rem(me + step, n)
        if not last:
            ref = half(right, 1) if step == n // 2 - 1 else piece(right)
            b = mail.send(ref, ref, minus)
            if arrived:
                arrived(right, None)
        elif arrived:
            arrived(right, 1)


def reduce_ring(mail, n, plus, minus, own, half, stage, land, delays, done):
    steps = n // 2
    a = mail.send(half(own(steps), 0), half(land(0, 1), 0), plus)
    b = mail.send(half(own(steps), 1), half(land(1, 1), 1), minus)
    for step in range(2, steps + 1):
        yield delays[step - 2]
        for way in (0, 1):
            mine = own(steps - step + 1 if way == 0 else n - steps + step - 1)
            (a, b)[way].wait_recv()
            came, out = land(way, step - 1), stage(way, step)
            if step == 2:
                half(out, way)[...] = (half(mine, way)[...].astype(F32) + half(came, way)[...].astype(F32)).astype(BF16)
                half(out, 1 - way)[...] = half(mine, 1 - way)[...]
            else:
                out[...] = (mine[...].astype(F32) + came[...].astype(F32)).astype(BF16)
            sent = mail.send(out, land(way, step), minus if way else plus)
            if way == 0:
                a = sent
            else:
                b = sent
    yield delays[steps - 1]
    mine = own(0)
    a.wait_recv()
    b.wait_recv()
    done(mine[...].astype(F32) + land(0, steps)[...].astype(F32) + land(1, steps)[...].astype(F32))


def halves(ref, h):
    return ref.at[pl.ds(h * 32, 32), :]


def reduce_tokens(mail, p, make, part, rs, pair, stage, land, done, times):
    other = 1 - p.c
    sends = {}
    ys = [lax.rem(p.y + o, Y) for o in range(Y)]
    for two in ((2, 1), (3, 0)):
        make([ys[o] for o in two])
        for o in two:
            sends[o] = mail.send(part(ys[o] * C + other), rs.at[ys[o]], p.sibling())
        yield 0.2
    plus, minus = p.along("y", 1), p.along("y", -1)
    yield times[0]

    def fold(o):
        sends[o].wait_recv()
        pair[ys[o]] = (part(ys[o] * C + p.c)[...].astype(F32) + rs[ys[o]].astype(F32)).astype(BF16)

    fold(2)
    a = mail.send(halves(pair.at[ys[2]], 0), land.at[0, 0], plus)
    b = mail.send(halves(pair.at[ys[2]], 1), land.at[1, 0], minus)
    fold(1)
    a1 = mail.send(halves(pair.at[ys[1]], 1), land.at[0, 1], plus)
    fold(3)
    b1 = mail.send(halves(pair.at[ys[3]], 0), land.at[1, 1], minus)
    fold(0)
    yield times[1]
    a.wait_recv()
    stage[0] = (pair[ys[1], 0:32].astype(F32) + land[0, 0].astype(F32)).astype(BF16)
    a2 = mail.send(stage.at[0], land.at[0, 2], plus)
    b.wait_recv()
    stage[1] = (pair[ys[3], 32:64].astype(F32) + land[1, 0].astype(F32)).astype(BF16)
    b2 = mail.send(stage.at[1], land.at[1, 2], minus)
    yield times[2]
    for copy in (a1, b1, a2, b2):
        copy.wait_recv()
    top = pair[ys[0], 0:32].astype(F32) + land[0, 2].astype(F32) + land[1, 1].astype(F32)
    low = pair[ys[0], 32:64].astype(F32) + land[0, 1].astype(F32) + land[1, 2].astype(F32)
    done(jnp.concatenate([top, low], axis=0))


SQ = math.sqrt(2.0 / math.pi)
FAR_FIRST = (4, 3, 5, 2, 6, 1, 7, 0)
FB = WIDTH // BLK


def rows64(ref, h):
    return ref.at[pl.ds(h * 64, 64), :]


def step_kernel(scale, x_ref, up_ref, gain_ref, win_ref, wout_ref, bi_ref, seg_ref, teacher_ref, readout_ref,
                lo_ref, ig_ref, gin_ref, gout_ref,
                x_v, gain_v, table_v, nrm_all, up_all, win_all, wout_all, bi_all, bi,
                nrm_blocks, act_rows, act_t, slope, wide_out, wide_in, part,
                rs1, pair1, stage1, land1, ids, scores, coeffs,
                cot, pre, back, din, dout, rs, pair, stage, land,
                za_stage, za_land, za_sum, xb_land, xb_sum, zb_stage, zb_land,
                slab, dealt_in, dealt, send_sem, recv_sem, local_sem):
    p = Place()
    mail = Mail(send_sem, recv_sem)
    flows = Flows()
    local = []

    def keep(src, dst):
        copy = pltpu.make_async_copy(src, dst, local_sem.at[len(local)])
        copy.start()
        local.append(copy)
        return copy

    yplus, yminus = p.along("y", 1), p.along("y", -1)
    zplus, zminus = p.along("z", 1), p.along("z", -1)
    near = [p.flat(1), p.flat(-1)]
    eye = lax.broadcasted_iota(jnp.int32, (ROWS, BLK), 0) == lax.broadcasted_iota(jnp.int32, (ROWS, BLK), 1)
    loads = [keep(x_ref, x_v), keep(gain_ref, gain_v), keep(bi_ref, table_v), keep(up_ref, up_all.at[p.q])]

    def first():
        for copy in loads[:3]:
            copy.wait()
        wide = x_v[...].astype(F32)
        inv_rms = lax.rsqrt(jnp.mean(wide * wide, axis=1, keepdims=True) + EPS)
        nrm_all[p.q] = (wide * inv_rms * gain_v[...]).astype(BF16)
        bi_all[p.z] = jnp.zeros((8, BLK), jnp.int32)
        bi_all[p.z, 0:KB, 0:Z] = table_v[...]
        ids[0] = jnp.full((8, BLK), -1.0, F32)
        ids[0, 0:1, 0:ROWS] = seg_ref[...].astype(F32)
        loads[3].wait()

    greet([p.plane(dx, o) for dx in range(X) for o in range(Q) if dx or o] + [zplus, zminus] + near, first)
    id_copies = [mail.send(ids.at[0], ids.at[1 + i], near[i]) for i in (0, 1)]

    def columns(ref, q):
        return ref.at[:, pl.ds(pl.multiple_of(q * BLK, BLK), BLK)]

    def my_rows(ref):
        return ref.at[pl.ds(pl.multiple_of(p.q * 16, 16), 16), :]

    in_slab, out_slab = win_all.at[p.z, p.x], wout_all.at[p.x, p.z]
    in_deals, out_deals = {}, []
    for o in range(Q):
        q = lax.rem(p.q + o, Q)
        for dx in range(X):
            if dx or o:
                in_deals[dx, o] = mail.send(columns(win_ref, q), my_rows(in_slab), p.plane(dx, o))
        if o:
            out_deals.append(mail.send(columns(wout_ref, q), my_rows(out_slab), p.member(o)))
    slab_copies = [keep(columns(win_ref, p.q), my_rows(in_slab)), keep(columns(wout_ref, p.q), my_rows(out_slab))]

    def tokens(out, first):
        def half(y, h):
            return out.at[y * C + p.c, pl.ds(h * 32, 32), :]

        relays = []

        def pass_on(ref, to):
            relays.append(mail.send(ref, ref, to))
            return relays[-1]

        a0 = mail.send(half(p.y, 0), half(p.y, 0), yplus)
        b1 = mail.send(half(p.y, 1), half(p.y, 1), yminus)
        a1 = mail.send(half(p.y, 1), half(p.y, 1), yplus)
        b0 = mail.send(half(p.y, 0), half(p.y, 0), yminus)
        pass_on(out.at[p.q], p.sibling())
        left, right, far = lax.rem(p.y + 3, Y), lax.rem(p.y + 1, Y), lax.rem(p.y + 2, Y)
        yield first
        a0.wait_recv()
        fa = mail.send(half(left, 0), half(left, 0), yplus)
        pass_on(half(left, 0), p.sibling())
        b1.wait_recv()
        fb = mail.send(half(right, 1), half(right, 1), yminus)
        pass_on(half(right, 1), p.sibling())
        yield 3.0
        a1.wait_recv()
        pass_on(half(left, 1), p.sibling())
        b0.wait_recv()
        pass_on(half(right, 0), p.sibling())
        yield 8.3
        fa.wait_recv()
        pass_on(half(far, 0), p.sibling())
        fb.wait_recv()
        pass_on(half(far, 1), p.sibling())
        yield 2.0
        for copy in relays:
            copy.wait_recv()

    def table():
        mine = bi_all.at[p.z]
        a = mail.send(mine, mine, zplus)
        b = mail.send(mine, mine, zminus)
        for step in range(1, Z // 2 + 1):
            yield 2.5
            a.wait_recv()
            left = bi_all.at[lax.rem(p.z - step + Z, Z)]
            if step < Z // 2:
                a = mail.send(left, left, zplus)
                b.wait_recv()
                right = bi_all.at[lax.rem(p.z + step, Z)]
                if step < Z // 2 - 1:
                    b = mail.send(right, right, zminus)
        known = pltpu.make_async_copy(bi_all, bi, local_sem.at[7])
        known.start()
        known.wait()

    def w_in_z(k):
        return gather_ring(
            mail, Z, p.z, zplus, zminus,
            lambda z: win_all.at[z, k],
            lambda z, h: win_all.at[z, k, pl.ds(h * 64, 64), :],
            [3.0] * 4)

    def w_out_x(z):
        ref = wout_all.at[p.x, z]
        copies = [mail.send(ref, ref, p.along("x", dx)) for dx in (1, 2, 3)]
        yield 6.0
        for copy in copies:
            copy.wait_recv()

    def w_in():
        yield 2.5
        slab_copies[0].wait()
        for dx in range(X):
            for o in range(Q):
                if dx or o:
                    in_deals[dx, o].wait_recv()
            flows.add(w_in_z(lax.rem(p.x - dx + X, X)), ("w_in", dx))
            yield 0.3

    def w_out():
        yield 2.6
        slab_copies[1].wait()
        for copy in out_deals:
            copy.wait_recv()
        seen, begun = [], []

        def got(z, h):
            if h is not None:
                seen.append(h)
            if h is None or len(seen) == 2:
                begun.append(z)
                flows.add(w_out_x(z), ("w_out", len(begun)))

        flows.add(gather_ring(
            mail, Z, p.z, zplus, zminus,
            lambda z: wout_all.at[p.x, z],
            lambda z, h: wout_all.at[p.x, z, pl.ds(h * 64, 64), :],
            [2.5] * 4, got))
        flows.add(w_out_x(p.z), ("w_out", 0))


    def member_rows(y):
        return pl.ds(pl.multiple_of(y * (C * ROWS), C * ROWS), C * ROWS)

    def member(ref):
        return lambda q: ref.at[pl.ds(pl.multiple_of(q * ROWS, ROWS), ROWS), :]

    def widen(j, blocks, out):
        at = [bi[j, k, p.q] for k in range(KB)]
        cols = slice(j * BLK, (j + 1) * BLK)
        for d in range(FB):
            out[d * BLK:(d + 1) * BLK, cols] = sum(
                blocks[k] * (at[k] == d).astype(F32).astype(BF16) for k in range(KB))

    def product(lhs, wide, out):
        def make(ys):
            rows = jnp.concatenate([lhs[member_rows(y), :] for y in ys], axis=0)
            for n in range(4):
                cols = slice(n * 512, (n + 1) * 512)
                value = dot(rows, wide[cols, :], NT).astype(BF16)
                for i, y in enumerate(ys):
                    out[member_rows(y), cols] = value[i * C * ROWS:(i + 1) * C * ROWS]
        return make

    total = []

    def forward():
        for d in range(FB):
            nrm_blocks[d] = nrm_all[:, :, d * BLK:(d + 1) * BLK].reshape(Q * ROWS, BLK)
        for j in range(Z):
            at = [bi[j, k, p.q] for k in range(KB)]
            picked = jnp.concatenate([nrm_blocks[a] for a in at], axis=1)
            v = dot(picked, win_all[j].reshape(KB * BLK, BLK), NN)
            tanh = jnp.tanh(SQ * (v + 0.044715 * (v * v * v)))
            act = 0.5 * v * (1.0 + tanh)
            slope[j] = 0.5 * (1.0 + tanh) + 0.5 * v * (1.0 - tanh * tanh) * (SQ * (1.0 + 3.0 * 0.044715 * (v * v)))
            act_rows[:, j * BLK:(j + 1) * BLK] = act.astype(BF16)
            act_t[j] = act.T.astype(BF16)
            widen(j, [wout_all[k, j] for k in range(KB)], wide_out)
            yield 0.7
        yield from reduce_tokens(
            mail, p, product(act_rows, wide_out, part), member(part), rs1, pair1, stage1, land1,
            total.append, [1.0, 4.0, 4.0])

    def wide_weights():
        for j in range(Z):
            yield 0.4
            widen(j, [win_all[j, k] for k in range(KB)], wide_in)

    def score():
        lo = (x_v[...].astype(F32) + total[0]).astype(BF16)
        lo_ref[...] = lo
        token = jnp.sum(lo.astype(F32) * readout_ref[...], axis=1, keepdims=True)
        scores[0] = jnp.broadcast_to(jnp.sum(jnp.where(eye, token, 0.0), axis=0, keepdims=True), (8, BLK))
        copies = [mail.send(scores.at[0], scores.at[1 + i], near[i]) for i in (0, 1)]
        ids_col = jnp.sum(jnp.where(eye, ids[0, 0:1, :], 0.0), axis=1, keepdims=True)
        segs = teacher_ref.shape[1]
        hot = lax.broadcasted_iota(jnp.int32, (ROWS, segs), 1).astype(F32) == ids_col
        teacher = jnp.sum(jnp.where(hot, teacher_ref[...], 0.0), axis=1, keepdims=True)
        yield 2.5
        for copy in id_copies + copies:
            copy.wait_recv()
        sums = jnp.zeros((ROWS, 1), F32)
        counts = jnp.zeros((ROWS, 1), F32)
        for i in range(3):
            same = ids[i, 0:1, :] == ids_col
            sums += jnp.sum(jnp.where(same, scores[i, 0:1, :], 0.0), axis=1, keepdims=True)
            counts += jnp.sum(jnp.where(same, 1.0, 0.0), axis=1, keepdims=True)
        coeff = (2.0 * LOSS_WEIGHT) * (sums / counts - teacher)
        coeff_row = jnp.sum(jnp.where(eye, coeff, 0.0), axis=0, keepdims=True)
        coeffs[p.q] = jnp.broadcast_to(coeff_row, (8, BLK))
        out = [mail.send(coeffs.at[p.q], coeffs.at[p.q], p.member(o)) for o in range(1, Q)]
        yield 2.5
        for copy in out:
            copy.wait_recv()

    def cotangent(b):
        coeff = jnp.sum(jnp.where(eye, coeffs[b][0:1, :], 0.0), axis=1, keepdims=True)
        return (up_all[b].astype(F32) + coeff * readout_ref[...]).astype(BF16)

    def block(dz):
        j = lax.rem(p.z + dz, Z)
        at = [bi[j, k, p.q] for k in range(KB)]
        picked = jnp.concatenate([cot[a] for a in at], axis=1)
        chosen = jnp.concatenate([nrm_blocks[a] for a in at], axis=1)
        w_out = jnp.concatenate([wout_all[k, j] for k in range(KB)], axis=0)
        value = dot(picked, w_out, NN) * slope[j]
        pre[:, pl.ds(pl.multiple_of(j * BLK, BLK), BLK)] = value.astype(BF16)
        d_in = (dot(value.T.astype(BF16), chosen, NN) * scale).astype(BF16)
        d_out = (dot(act_t[j], picked, NN) * scale).astype(BF16)
        for k in range(KB):
            cols = slice(k * BLK, (k + 1) * BLK)
            din[dz, k] = d_in[:, cols]
            dout[dz, k] = d_out[:, cols]

    ready = set()
    grads, deals, x_sends = [], [], {}

    def out_x(dz):
        for dx in (1, 2, 3):
            x = lax.rem(p.x + dx, X)
            x_sends[dz, dx] = mail.send(dout.at[dz, x], xb_land.at[dx - 1, dz], p.along("x", dx))

    def in_z(dx):
        k = lax.rem(p.x + dx, X)

        def own(dz):
            assert dz in ready
            return din.at[dz, k]

        def done(value):
            za_sum[dx] = value.T.astype(BF16)
            for o in range(Q):
                rows = pl.ds(pl.multiple_of(lax.rem(p.q + o, Q) * 16, 16), 16)
                if dx == 0 and o == 0:
                    dealt_in[p.x, p.q] = za_sum[dx, rows, :]
                else:
                    deals.append(mail.send(za_sum.at[dx, rows, :], dealt_in.at[p.x, p.q], p.plane(dx, o)))

        return reduce_ring(
            mail, Z, zplus, zminus, own, rows64,
            lambda way, step: za_stage.at[dx, way, step - 2], lambda way, step: za_land.at[dx, way, step - 1],
            [3.2] * 4, done)

    summed = set()

    def out_own(dz):
        if dz not in summed:
            assert dz in ready
            summed.add(dz)
            for dx in (1, 2, 3):
                x_sends[dz, dx].wait_recv()
            value = dout[dz, p.x].astype(F32) + sum(xb_land[i, dz].astype(F32) for i in range(3))
            xb_sum[dz] = value.astype(BF16)
        return xb_sum.at[dz]

    def deal(value):
        slab[...] = value.T.astype(BF16)
        dealt[p.q] = slab[pl.ds(pl.multiple_of(p.q * 16, 16), 16), :]
        for o in range(1, Q):
            rows = slab.at[pl.ds(pl.multiple_of(lax.rem(p.q + o, Q) * 16, 16), 16), :]
            deals.append(mail.send(rows, dealt.at[p.q], p.member(o)))

    def out_z():
        yield 3.5
        yield from reduce_ring(
            mail, Z, zplus, zminus, out_own, rows64,
            lambda way, step: zb_stage.at[way, step - 2], lambda way, step: zb_land.at[way, step - 1],
            [3.0, 3.0, 3.0, 3.0], deal)

    def compute():
        for b in range(Q):
            value = cotangent(b)
            for d in range(FB):
                cot[d, b * ROWS:(b + 1) * ROWS, :] = value[:, d * BLK:(d + 1) * BLK]
        for dz in FAR_FIRST:
            block(dz)
            ready.add(dz)
            out_x(dz)
            if dz == FAR_FIRST[0]:
                for dx in (1, 2, 3, 0):
                    flows.add(in_z(dx))
                flows.add(out_z())
            yield 1.0
        yield from reduce_tokens(
            mail, p, product(pre, wide_in, back), member(back), rs, pair, stage, land,
            grads.append, [1.0, 5.0, 6.0])

    flows.add(w_in())
    flows.add(w_out())
    flows.add(tokens(nrm_all, 4.5), "normed")
    flows.add(tokens(up_all, 10.0), "upstream")
    flows.add(table(), "table")
    gathered = ["normed", "table"] + [("w_in", i) for i in range(X)] + [("w_out", i) for i in range(Z)]
    flows.after(gathered, lambda: (flows.add(forward(), "forward"), flows.add(wide_weights(), "wide")))
    flows.after(["forward"], lambda: flows.add(score(), "score"))
    flows.after(["score", "upstream", "wide"], lambda: flows.add(compute()))
    flows.run()

    wide = x_v[...].astype(F32)
    inv = lax.rsqrt(jnp.mean(wide * wide, axis=1, keepdims=True) + EPS)
    scaled = grads[0] * gain_v[...]
    inner = jnp.mean(scaled * wide, axis=1, keepdims=True)
    ig_ref[...] = (cotangent(p.q).astype(F32) + (inv * scaled - wide * (inv * inv * inv) * inner)).astype(BF16)
    for copy in deals:
        copy.wait_recv()
    for q in range(Q):
        cols = slice(q * BLK, (q + 1) * BLK)
        gin_ref[:, cols] = sum(dealt_in[x, q].astype(F32) for x in range(X))
        gout_ref[:, cols] = dealt[q].astype(F32)
    mail.close()


def step(scale, *arrays):
    n = Q * ROWS
    tile = (BLK, BLK)
    far = pl.BlockSpec(memory_space=pltpu.HBM)

    def token_buffers():
        return [
            pltpu.VMEM((Y, ROWS, WIDTH), BF16),
            pltpu.VMEM((Y, ROWS, WIDTH), BF16),
            pltpu.VMEM((2, ROWS // 2, WIDTH), BF16),
            pltpu.VMEM((2, 3, ROWS // 2, WIDTH), BF16),
        ]

    return pl.pallas_call(
        functools.partial(step_kernel, scale),
        name="step",
        out_shape=(
            jax.ShapeDtypeStruct((ROWS, WIDTH), BF16),
            jax.ShapeDtypeStruct((ROWS, WIDTH), BF16),
            jax.ShapeDtypeStruct((16, Q * BLK), F32),
            jax.ShapeDtypeStruct((16, Q * BLK), F32),
        ),
        in_specs=[far] * 6 + [VM] * 3,
        out_specs=(VM,) * 4,
        scratch_shapes=[
            pltpu.VMEM((ROWS, WIDTH), BF16),
            pltpu.VMEM((1, WIDTH), F32),
            pltpu.VMEM((KB, Z), jnp.int32),
            pltpu.VMEM((Q, ROWS, WIDTH), BF16),
            pltpu.VMEM((Q, ROWS, WIDTH), BF16),
            pltpu.VMEM((Z, KB) + tile, BF16),
            pltpu.VMEM((KB, Z) + tile, BF16),
            pltpu.VMEM((Z, 8, BLK), jnp.int32),
            pltpu.SMEM((Z, 8, BLK), jnp.int32),
            pltpu.VMEM((FB, n, BLK), BF16),
            pltpu.VMEM((n, Z * BLK), BF16),
            pltpu.VMEM((Z, BLK, n), BF16),
            pltpu.VMEM((Z, n, BLK), F32),
            pltpu.VMEM((WIDTH, Z * BLK), BF16),
            pltpu.VMEM((WIDTH, Z * BLK), BF16),
            pltpu.VMEM((n, WIDTH), BF16),
            *token_buffers(),
            pltpu.VMEM((3, 8, BLK), F32),
            pltpu.VMEM((3, 8, BLK), F32),
            pltpu.VMEM((Q, 8, BLK), F32),
            pltpu.VMEM((FB, n, BLK), BF16),
            pltpu.VMEM((n, Z * BLK), BF16),
            pltpu.VMEM((n, WIDTH), BF16),
            pltpu.VMEM((Z, KB) + tile, BF16),
            pltpu.VMEM((Z, KB) + tile, BF16),
            *token_buffers(),
            pltpu.VMEM((KB, 2, 3) + tile, BF16),
            pltpu.VMEM((KB, 2, 4) + tile, BF16),
            pltpu.VMEM((KB,) + tile, BF16),
            pltpu.VMEM((3, Z) + tile, BF16),
            pltpu.VMEM((Z,) + tile, BF16),
            pltpu.VMEM((2, 3) + tile, BF16),
            pltpu.VMEM((2, 4) + tile, BF16),
            pltpu.VMEM(tile, BF16),
            pltpu.VMEM((X, Q, 16, BLK), BF16),
            pltpu.VMEM((Q, 16, BLK), BF16),
            pltpu.SemaphoreType.DMA((288,)),
            pltpu.SemaphoreType.DMA((288,)),
            pltpu.SemaphoreType.DMA((8,)),
        ],
        compiler_params=pltpu.CompilerParams(collective_id=0, has_side_effects=True, vmem_limit_bytes=60 << 20),
    )(*arrays)


def on_device(
    inputs, norm_gain, w_in, w_out, block_index, segment_ids, teacher_scores, upstream, readout
):
    scale = 1.0 / math.sqrt(ROWS * X * Q * Z)
    remote = [pltpu.with_memory_space_constraint(a, pltpu.HBM)
              for a in (inputs, upstream, norm_gain[None, :], w_in, w_out, block_index.T)]
    return step(scale, *remote, segment_ids[None, :], teacher_scores[None, :], readout[None, :])


def solution(mesh):
    return jax.shard_map(
        on_device,
        mesh=mesh,
        in_specs=(
            P(("tok", "feat"), None),
            P(),
            P("tok", "feat"),
            P("tok", "feat"),
            P("feat", None),
            P(("tok", "feat")),
            P(),
            P(("tok", "feat"), None),
            P(),
        ),
        out_specs=(
            P(("tok", "feat"), None),
            P(("tok", "feat"), None),
            P("tok", "feat"),
            P("tok", "feat"),
        ),
        check_vma=False,
    )
```

```python
import functools
import heapq
import math

import jax
import jax.numpy as jnp
from jax import lax
from jax.experimental import pallas as pl
from jax.experimental.pallas import tpu as pltpu
from jax.sharding import PartitionSpec as P

BLK = 128
EPS = 1e-06
LOSS_WEIGHT = 8.0
X, Y, C, Z = 4, 4, 2, 8
Q = Y * C
ROWS = 64
WIDTH = 2048
KB = 4
SEGMENTS = 1024
MESH = pl.DeviceIdType.MESH
F32, BF16 = jnp.float32, jnp.bfloat16
NT = (((1,), (1,)), ((), ()))
NN = (((1,), (0,)), ((), ()))
VM = pl.BlockSpec(memory_space=pltpu.VMEM)
ANY = pl.BlockSpec(memory_space=pl.ANY)


def dot(a, b, dims):
    return lax.dot_general(a, b, dims, preferred_element_type=F32)


class Place:
    def __init__(self):
        t = lax.axis_index("tok")
        self.z = lax.axis_index("feat")
        self.t = t
        self.q = lax.rem(t, Q)
        self.c = lax.rem(t, C)
        self.y = lax.rem(t // C, Y)
        self.x = t // Q

    def at(self, x=None, y=None, c=None, z=None):
        x, y = self.x if x is None else x, self.y if y is None else y
        c, z = self.c if c is None else c, self.z if z is None else z
        return {"tok": (x * Y + y) * C + c, "feat": z}

    def sibling(self):
        return self.at(c=1 - self.c)

    def along(self, axis, by):
        n = {"x": X, "y": Y, "z": Z}[axis]
        me = {"x": self.x, "y": self.y, "z": self.z}[axis]
        return self.at(**{axis: lax.rem(me + by + n, n)})

    def member(self, by):
        return {"tok": self.x * Q + lax.rem(self.q + by + Q, Q), "feat": self.z}

    def plane(self, dx, by):
        return {"tok": lax.rem(self.x + dx + X, X) * Q + lax.rem(self.q + by + Q, Q), "feat": self.z}

    def flat(self, by):
        n = X * Q * Z
        d = lax.rem(self.t * Z + self.z + by + n, n)
        return {"tok": d // Z, "feat": lax.rem(d, Z)}


class Mail:
    def __init__(self, send_sem, recv_sem):
        self.send_sem, self.recv_sem, self.sent = send_sem, recv_sem, []

    def send(self, src, dst, to):
        i = len(self.sent)
        copy = pltpu.make_async_remote_copy(
            src_ref=src,
            dst_ref=dst,
            send_sem=self.send_sem.at[i],
            recv_sem=self.recv_sem.at[i],
            device_id=to,
            device_id_type=MESH,
        )
        copy.start()
        self.sent.append(copy)
        return copy

    def close(self):
        for copy in self.sent:
            copy.wait_send()


def greet(devices, meanwhile=None):
    barrier = pltpu.get_barrier_semaphore()
    for device in devices:
        pl.semaphore_signal(barrier, inc=1, device_id=device, device_id_type=MESH)
    if meanwhile:
        meanwhile()
    pl.semaphore_wait(barrier, len(devices))


class Flows:
    def __init__(self):
        self.heap, self.now, self.count = [], 0.0, 0
        self.ended, self.pending = set(), []

    def add(self, flow, name=None):
        heapq.heappush(self.heap, (self.now, self.count, flow, name))
        self.count += 1

    def after(self, names, start):
        self.pending.append((set(names), start))

    def end(self, name):
        self.ended.add(name)
        for names, start in list(self.pending):
            if names <= self.ended:
                self.pending.remove((names, start))
                start()

    def run(self):
        while self.heap:
            self.now, _, flow, name = heapq.heappop(self.heap)
            for delay in flow:
                heapq.heappush(self.heap, (self.now + delay, self.count, flow, name))
                self.count += 1
                break
            else:
                if name is not None:
                    self.end(name)
        assert not self.pending


def gather_ring(mail, n, me, plus, minus, piece, half, delays, arrived=None):
    a = mail.send(piece(me), piece(me), plus)
    b = mail.send(piece(me), piece(me), minus)
    for step in range(1, n // 2 + 1):
        yield delays[step - 1]
        last = step == n // 2
        a.wait_recv()
        left = lax.rem(me - step + n, n)
        if not last:
            ref = half(left, 0) if step == n // 2 - 1 else piece(left)
            a = mail.send(ref, ref, plus)
            if arrived:
                arrived(left, None, n - step)
        elif arrived:
            arrived(left, 0, n - step)
        b.wait_recv()
        right = lax.rem(me + step, n)
        if not last:
            ref = half(right, 1) if step == n // 2 - 1 else piece(right)
            b = mail.send(ref, ref, minus)
            if arrived:
                arrived(right, None, step)
        elif arrived:
            arrived(right, 1, step)


def reduce_ring(mail, n, plus, minus, own, half, stage, land, delays, done):
    steps = n // 2
    a = mail.send(half(own(steps), 0), half(land(0, 1), 0), plus)
    b = mail.send(half(own(steps), 1), half(land(1, 1), 1), minus)
    for step in range(2, steps + 1):
        yield delays[step - 2]
        for way in (0, 1):
            mine = own(steps - step + 1 if way == 0 else n - steps + step - 1)
            (a, b)[way].wait_recv()
            came, out = land(way, step - 1), stage(way, step)
            if step == 2:
                half(out, way)[...] = (half(mine, way)[...].astype(F32) + half(came, way)[...].astype(F32)).astype(BF16)
                half(out, 1 - way)[...] = half(mine, 1 - way)[...]
            else:
                out[...] = (mine[...].astype(F32) + came[...].astype(F32)).astype(BF16)
            sent = mail.send(out, land(way, step), minus if way else plus)
            if way == 0:
                a = sent
            else:
                b = sent
    yield delays[steps - 1]
    mine = own(0)
    a.wait_recv()
    b.wait_recv()
    done(mine[...].astype(F32) + land(0, steps)[...].astype(F32) + land(1, steps)[...].astype(F32))


def halves(ref, h):
    return ref.at[pl.ds(h * 32, 32), :]


def reduce_tokens(mail, p, make, part, rs, pair, stage, land, done, times):
    other = 1 - p.c
    sends = {}
    ys = [lax.rem(p.y + o, Y) for o in range(Y)]
    for two in ((2, 1, 3, 0),):
        yield from make([ys[o] for o in two])
        for o in two:
            sends[o] = mail.send(part(ys[o] * C + other), rs.at[ys[o]], p.sibling())
        yield 0.2
    plus, minus = p.along("y", 1), p.along("y", -1)
    yield times[0]

    def fold(o):
        sends[o].wait_recv()
        pair[ys[o]] = (part(ys[o] * C + p.c)[...].astype(F32) + rs[ys[o]].astype(F32)).astype(BF16)

    fold(2)
    a = mail.send(halves(pair.at[ys[2]], 0), land.at[0, 0], plus)
    b = mail.send(halves(pair.at[ys[2]], 1), land.at[1, 0], minus)
    fold(1)
    a1 = mail.send(halves(pair.at[ys[1]], 1), land.at[0, 1], plus)
    fold(3)
    b1 = mail.send(halves(pair.at[ys[3]], 0), land.at[1, 1], minus)
    fold(0)
    yield times[1]
    a.wait_recv()
    stage[0] = (pair[ys[1], 0:32].astype(F32) + land[0, 0].astype(F32)).astype(BF16)
    a2 = mail.send(stage.at[0], land.at[0, 2], plus)
    b.wait_recv()
    stage[1] = (pair[ys[3], 32:64].astype(F32) + land[1, 0].astype(F32)).astype(BF16)
    b2 = mail.send(stage.at[1], land.at[1, 2], minus)
    yield times[2]
    for copy in (a1, b1, a2, b2):
        copy.wait_recv()
    top = pair[ys[0], 0:32].astype(F32) + land[0, 2].astype(F32) + land[1, 1].astype(F32)
    low = pair[ys[0], 32:64].astype(F32) + land[0, 1].astype(F32) + land[1, 2].astype(F32)
    done(jnp.concatenate([top, low], axis=0))


SQ = math.sqrt(2.0 / math.pi)
FAR_FIRST = (4, 3, 5, 2, 6, 1, 7, 0)
FB = WIDTH // BLK


def rows64(ref, h):
    return ref.at[pl.ds(h * 64, 64), :]


def step_kernel(scale, x_ref, up_ref, gain_ref, win_ref, wout_ref, bi_ref, seg_hbm, teacher_hbm, readout_hbm,
                lo_ref, ig_ref, gin_ref, gout_ref,
                x_v, gain_v, table_v, seg_ref, teacher_ref, readout_ref, nrm_all, up_all, win_all, wout_all, bi_all, bi,
                nrm_blocks, act_rows, act_t, slope, wide_out, wide_in, part,
                rs1, pair1, stage1, land1, ids, scores, coeffs,
                cot, pre, back, din, dout, rs, pair, stage, land,
                za_stage, za_land, za_sum, xb_land, xb_sum, zb_stage, zb_land,
                slab, dealt_in, dealt, send_sem, recv_sem, local_sem):
    p = Place()
    mail = Mail(send_sem, recv_sem)
    flows = Flows()
    local = []

    def keep(src, dst):
        copy = pltpu.make_async_copy(src, dst, local_sem.at[len(local)])
        copy.start()
        local.append(copy)
        return copy

    yplus, yminus = p.along("y", 1), p.along("y", -1)
    zplus, zminus = p.along("z", 1), p.along("z", -1)
    near = [p.flat(1), p.flat(-1)]
    eye = lax.broadcasted_iota(jnp.int32, (ROWS, BLK), 0) == lax.broadcasted_iota(jnp.int32, (ROWS, BLK), 1)
    loads = [keep(x_ref, x_v), keep(gain_ref, gain_v), keep(bi_ref, table_v), keep(seg_hbm, seg_ref),
             keep(teacher_hbm, teacher_ref), keep(readout_hbm, readout_ref), keep(up_ref, up_all.at[p.q])]

    def first():
        for copy in loads[:4]:
            copy.wait()
        wide = x_v[...].astype(F32)
        inv_rms = lax.rsqrt(jnp.mean(wide * wide, axis=1, keepdims=True) + EPS)
        nrm_all[p.q] = (wide * inv_rms * gain_v[...]).astype(BF16)
        bi_all[p.z] = jnp.zeros((8, BLK), jnp.int32)
        bi_all[p.z, 0:KB, 0:Z] = table_v[...]
        ids[0] = jnp.full((8, BLK), -1.0, F32)
        ids[0, 0:1, 0:ROWS] = seg_ref[...].astype(F32)
        for copy in loads[4:]:
            copy.wait()

    greet([p.plane(dx, o) for dx in range(X) for o in range(Q) if dx or o] + [zplus, zminus] + near, first)
    id_copies = [mail.send(ids.at[0], ids.at[1 + i], near[i]) for i in (0, 1)]

    def columns(ref, q):
        return ref.at[:, pl.ds(pl.multiple_of(q * BLK, BLK), BLK)]

    def my_rows(ref):
        return ref.at[pl.ds(pl.multiple_of(p.q * 16, 16), 16), :]

    in_slab, out_slab = win_all.at[p.z, p.x], wout_all.at[p.x, p.z]
    in_deals, out_deals = {}, []
    for o in range(Q):
        q = lax.rem(p.q + o, Q)
        for dx in range(X):
            if dx or o:
                in_deals[dx, o] = mail.send(columns(win_ref, q), my_rows(in_slab), p.plane(dx, o))
        if o:
            out_deals.append(mail.send(columns(wout_ref, q), my_rows(out_slab), p.member(o)))
    slab_copies = [keep(columns(win_ref, p.q), my_rows(in_slab)), keep(columns(wout_ref, p.q), my_rows(out_slab))]

    def tokens(out, first):
        def half(y, h):
            return out.at[y * C + p.c, pl.ds(h * 32, 32), :]

        relays = []

        def pass_on(ref, to):
            relays.append(mail.send(ref, ref, to))
            return relays[-1]

        a0 = mail.send(half(p.y, 0), half(p.y, 0), yplus)
        b1 = mail.send(half(p.y, 1), half(p.y, 1), yminus)
        a1 = mail.send(half(p.y, 1), half(p.y, 1), yplus)
        b0 = mail.send(half(p.y, 0), half(p.y, 0), yminus)
        pass_on(out.at[p.q], p.sibling())
        left, right, far = lax.rem(p.y + 3, Y), lax.rem(p.y + 1, Y), lax.rem(p.y + 2, Y)
        yield first
        a0.wait_recv()
        fa = mail.send(half(left, 0), half(left, 0), yplus)
        pass_on(half(left, 0), p.sibling())
        b1.wait_recv()
        fb = mail.send(half(right, 1), half(right, 1), yminus)
        pass_on(half(right, 1), p.sibling())
        yield 3.0
        a1.wait_recv()
        pass_on(half(left, 1), p.sibling())
        b0.wait_recv()
        pass_on(half(right, 0), p.sibling())
        yield 8.3
        fa.wait_recv()
        pass_on(half(far, 0), p.sibling())
        fb.wait_recv()
        pass_on(half(far, 1), p.sibling())
        yield 2.0
        for copy in relays:
            copy.wait_recv()

    def table():
        mine = bi_all.at[p.z]
        a = mail.send(mine, mine, zplus)
        b = mail.send(mine, mine, zminus)
        for step in range(1, Z // 2 + 1):
            yield 2.5
            a.wait_recv()
            left = bi_all.at[lax.rem(p.z - step + Z, Z)]
            if step < Z // 2:
                a = mail.send(left, left, zplus)
                b.wait_recv()
                right = bi_all.at[lax.rem(p.z + step, Z)]
                if step < Z // 2 - 1:
                    b = mail.send(right, right, zminus)
        known = pltpu.make_async_copy(bi_all, bi, local_sem.at[11])
        known.start()
        known.wait()

    arrivals = {}

    def got_in(z, h, d):
        arrivals[d] = arrivals.get(d, 0) + 1
        if arrivals[d] == (KB if h is None else 2 * KB):
            flows.end(("w_in", d))

    def w_in_z(k):
        return gather_ring(
            mail, Z, p.z, zplus, zminus,
            lambda z: win_all.at[z, k],
            lambda z, h: win_all.at[z, k, pl.ds(h * 64, 64), :],
            [3.0] * 4, got_in)

    def w_out_x(z):
        ref = wout_all.at[p.x, z]
        copies = [mail.send(ref, ref, p.along("x", dx)) for dx in (1, 2, 3)]
        yield 6.0
        for copy in copies:
            copy.wait_recv()

    def w_in():
        yield 2.5
        slab_copies[0].wait()
        for dx in range(X):
            for o in range(Q):
                if dx or o:
                    in_deals[dx, o].wait_recv()
            flows.add(w_in_z(lax.rem(p.x - dx + X, X)))
            yield 0.3
        flows.end(("w_in", 0))

    def w_out():
        yield 2.6
        slab_copies[1].wait()
        for copy in out_deals:
            copy.wait_recv()
        seen = []

        def got(z, h, d):
            if h is not None:
                seen.append(h)
            if h is None or len(seen) == 2:
                flows.add(w_out_x(z), ("w_out", d))

        flows.add(gather_ring(
            mail, Z, p.z, zplus, zminus,
            lambda z: wout_all.at[p.x, z],
            lambda z, h: wout_all.at[p.x, z, pl.ds(h * 64, 64), :],
            [2.5] * 4, got))
        flows.add(w_out_x(p.z), ("w_out", 0))


    def member_rows(y):
        return pl.ds(pl.multiple_of(y * (C * ROWS), C * ROWS), C * ROWS)

    def member(ref):
        return lambda q: ref.at[pl.ds(pl.multiple_of(q * ROWS, ROWS), ROWS), :]

    def widen(j, blocks, out):
        at = [bi[lax.rem(p.z + j, Z), k, p.q] for k in range(KB)]
        cols = slice(j * BLK, (j + 1) * BLK)
        for d in range(FB):
            out[d * BLK:(d + 1) * BLK, cols] = sum(
                blocks[k] * (at[k] == d).astype(F32).astype(BF16) for k in range(KB))

    def product(lhs, wide, out):
        def make(ys):
            rows = jnp.concatenate([lhs[member_rows(y), :] for y in ys], axis=0)
            for n in range(4):
                cols = slice(n * 512, (n + 1) * 512)
                value = dot(rows, wide[cols, :], NT).astype(BF16)
                for i, y in enumerate(ys):
                    out[member_rows(y), cols] = value[i * C * ROWS:(i + 1) * C * ROWS]
                yield 0.5
        return make

    total = []

    def blocks():
        for d in range(FB):
            nrm_blocks[d] = nrm_all[:, :, d * BLK:(d + 1) * BLK].reshape(Q * ROWS, BLK)
        yield 0.3

    def forward_block(d):
        j = lax.rem(p.z + d, Z)
        at = [bi[j, k, p.q] for k in range(KB)]
        picked = jnp.concatenate([nrm_blocks[a] for a in at], axis=1)
        v = dot(picked, win_all[j].reshape(KB * BLK, BLK), NN)
        tanh = jnp.tanh(SQ * (v + 0.044715 * (v * v * v)))
        act = 0.5 * v * (1.0 + tanh)
        slope[d] = 0.5 * (1.0 + tanh) + 0.5 * v * (1.0 - tanh * tanh) * (SQ * (1.0 + 3.0 * 0.044715 * (v * v)))
        act_rows[:, d * BLK:(d + 1) * BLK] = act.astype(BF16)
        act_t[d] = act.T.astype(BF16)
        yield 0.5
        widen(d, [wout_all[k, j] for k in range(KB)], wide_out)
        yield 0.3

    def forward():
        yield from reduce_tokens(
            mail, p, product(act_rows, wide_out, part), member(part), rs1, pair1, stage1, land1,
            total.append, [1.0, 4.0, 4.0])

    def wide_weights():
        yield 4.5
        for d in range(Z):
            widen(d, [win_all[lax.rem(p.z + d, Z), k] for k in range(KB)], wide_in)
            yield 0.4

    def score():
        lo = (x_v[...].astype(F32) + total[0]).astype(BF16)
        lo_ref[...] = lo
        token = jnp.sum(lo.astype(F32) * readout_ref[...], axis=1, keepdims=True)
        scores[0] = jnp.broadcast_to(jnp.sum(jnp.where(eye, token, 0.0), axis=0, keepdims=True), (8, BLK))
        copies = [mail.send(scores.at[0], scores.at[1 + i], near[i]) for i in (0, 1)]
        ids_col = jnp.sum(jnp.where(eye, ids[0, 0:1, :], 0.0), axis=1, keepdims=True)
        segs = teacher_ref.shape[1]
        hot = lax.broadcasted_iota(jnp.int32, (ROWS, segs), 1).astype(F32) == ids_col
        teacher = jnp.sum(jnp.where(hot, teacher_ref[...], 0.0), axis=1, keepdims=True)
        yield 2.5
        for copy in id_copies + copies:
            copy.wait_recv()
        sums = jnp.zeros((ROWS, 1), F32)
        counts = jnp.zeros((ROWS, 1), F32)
        for i in range(3):
            same = ids[i, 0:1, :] == ids_col
            sums += jnp.sum(jnp.where(same, scores[i, 0:1, :], 0.0), axis=1, keepdims=True)
            counts += jnp.sum(jnp.where(same, 1.0, 0.0), axis=1, keepdims=True)
        coeff = (2.0 * LOSS_WEIGHT) * (sums / counts - teacher)
        coeff_row = jnp.sum(jnp.where(eye, coeff, 0.0), axis=0, keepdims=True)
        coeffs[p.q] = jnp.broadcast_to(coeff_row, (8, BLK))
        out = [mail.send(coeffs.at[p.q], coeffs.at[p.q], p.member(o)) for o in range(1, Q)]
        yield 2.5
        for copy in out:
            copy.wait_recv()

    def cotangent(b):
        coeff = jnp.sum(jnp.where(eye, coeffs[b][0:1, :], 0.0), axis=1, keepdims=True)
        return (up_all[b].astype(F32) + coeff * readout_ref[...]).astype(BF16)

    def block(dz):
        j = lax.rem(p.z + dz, Z)
        at = [bi[j, k, p.q] for k in range(KB)]
        picked = jnp.concatenate([cot[a] for a in at], axis=1)
        chosen = jnp.concatenate([nrm_blocks[a] for a in at], axis=1)
        w_out = jnp.concatenate([wout_all[k, j] for k in range(KB)], axis=0)
        value = dot(picked, w_out, NN) * slope[dz]
        pre[:, dz * BLK:(dz + 1) * BLK] = value.astype(BF16)
        yield 0.4
        d_in = (dot(value.T.astype(BF16), chosen, NN) * scale).astype(BF16)
        yield 0.3
        d_out = (dot(act_t[dz], picked, NN) * scale).astype(BF16)
        for k in range(KB):
            cols = slice(k * BLK, (k + 1) * BLK)
            din[dz, k] = d_in[:, cols]
            dout[dz, k] = d_out[:, cols]

    ready = set()
    grads, deals, x_sends = [], [], {}

    def out_x(dz):
        for dx in (1, 2, 3):
            x = lax.rem(p.x + dx, X)
            x_sends[dz, dx] = mail.send(dout.at[dz, x], xb_land.at[dx - 1, dz], p.along("x", dx))

    def in_z(dx):
        k = lax.rem(p.x + dx, X)

        def own(dz):
            assert dz in ready
            return din.at[dz, k]

        def done(value):
            za_sum[dx] = value.T.astype(BF16)
            for o in range(Q):
                rows = pl.ds(pl.multiple_of(lax.rem(p.q + o, Q) * 16, 16), 16)
                if dx == 0 and o == 0:
                    dealt_in[p.x, p.q] = za_sum[dx, rows, :]
                else:
                    deals.append(mail.send(za_sum.at[dx, rows, :], dealt_in.at[p.x, p.q], p.plane(dx, o)))

        return reduce_ring(
            mail, Z, zplus, zminus, own, rows64,
            lambda way, step: za_stage.at[dx, way, step - 2], lambda way, step: za_land.at[dx, way, step - 1],
            [4.5] * 4, done)

    summed = set()

    def out_own(dz):
        if dz not in summed:
            assert dz in ready
            summed.add(dz)
            for dx in (1, 2, 3):
                x_sends[dz, dx].wait_recv()
            value = dout[dz, p.x].astype(F32) + sum(xb_land[i, dz].astype(F32) for i in range(3))
            xb_sum[dz] = value.astype(BF16)
        return xb_sum.at[dz]

    def deal(value):
        slab[...] = value.T.astype(BF16)
        dealt[p.q] = slab[pl.ds(pl.multiple_of(p.q * 16, 16), 16), :]
        for o in range(1, Q):
            rows = slab.at[pl.ds(pl.multiple_of(lax.rem(p.q + o, Q) * 16, 16), 16), :]
            deals.append(mail.send(rows, dealt.at[p.q], p.member(o)))

    def out_z():
        yield 3.5
        yield from reduce_ring(
            mail, Z, zplus, zminus, out_own, rows64,
            lambda way, step: zb_stage.at[way, step - 2], lambda way, step: zb_land.at[way, step - 1],
            [4.0] * 4, deal)

    def compute():
        for b in range(Q):
            value = cotangent(b)
            for d in range(FB):
                cot[d, b * ROWS:(b + 1) * ROWS, :] = value[:, d * BLK:(d + 1) * BLK]
        for dz in FAR_FIRST:
            yield from block(dz)
            ready.add(dz)
            out_x(dz)
            if dz == FAR_FIRST[0]:
                for dx in (1, 2, 3, 0):
                    flows.add(in_z(dx))
                flows.add(out_z())
            yield 0.3
        yield from reduce_tokens(
            mail, p, product(pre, wide_in, back), member(back), rs, pair, stage, land,
            grads.append, [1.0, 5.0, 6.0])

    flows.add(w_in())
    flows.add(w_out())
    flows.add(tokens(nrm_all, 4.5), "normed")
    flows.add(tokens(up_all, 10.0), "upstream")
    flows.add(table(), "table")
    flows.after(["normed"], lambda: flows.add(blocks(), "blocks"))
    for d in range(Z):
        flows.after(["blocks", "table", ("w_in", d), ("w_out", d)],
                    lambda d=d: flows.add(forward_block(d), ("act", d)))
    flows.after([("act", d) for d in range(Z)],
                lambda: (flows.add(forward(), "forward"), flows.add(wide_weights(), "wide")))
    flows.after(["forward"], lambda: flows.add(score(), "score"))
    flows.after(["score", "upstream", "wide"], lambda: flows.add(compute()))
    flows.run()

    wide = x_v[...].astype(F32)
    inv = lax.rsqrt(jnp.mean(wide * wide, axis=1, keepdims=True) + EPS)
    scaled = grads[0] * gain_v[...]
    inner = jnp.mean(scaled * wide, axis=1, keepdims=True)
    ig_ref[...] = (cotangent(p.q).astype(F32) + (inv * scaled - wide * (inv * inv * inv) * inner)).astype(BF16)
    for copy in deals:
        copy.wait_recv()
    for q in range(Q):
        cols = slice(q * BLK, (q + 1) * BLK)
        gin_ref[:, cols] = sum(dealt_in[x, q].astype(F32) for x in range(X))
        gout_ref[:, cols] = dealt[q].astype(F32)
    mail.close()


def step(scale, *arrays):
    n = Q * ROWS
    tile = (BLK, BLK)
    far = pl.BlockSpec(memory_space=pltpu.HBM)

    def token_buffers():
        return [
            pltpu.VMEM((Y, ROWS, WIDTH), BF16),
            pltpu.VMEM((Y, ROWS, WIDTH), BF16),
            pltpu.VMEM((2, ROWS // 2, WIDTH), BF16),
            pltpu.VMEM((2, 3, ROWS // 2, WIDTH), BF16),
        ]

    return pl.pallas_call(
        functools.partial(step_kernel, scale),
        name="step",
        out_shape=(
            jax.ShapeDtypeStruct((ROWS, WIDTH), BF16),
            jax.ShapeDtypeStruct((ROWS, WIDTH), BF16),
            jax.ShapeDtypeStruct((16, Q * BLK), F32),
            jax.ShapeDtypeStruct((16, Q * BLK), F32),
        ),
        in_specs=[far] * 9,
        out_specs=(VM,) * 4,
        scratch_shapes=[
            pltpu.VMEM((ROWS, WIDTH), BF16),
            pltpu.VMEM((1, WIDTH), F32),
            pltpu.VMEM((KB, Z), jnp.int32),
            pltpu.VMEM((1, ROWS), jnp.int32),
            pltpu.VMEM((1, SEGMENTS), F32),
            pltpu.VMEM((1, WIDTH), F32),
            pltpu.VMEM((Q, ROWS, WIDTH), BF16),
            pltpu.VMEM((Q, ROWS, WIDTH), BF16),
            pltpu.VMEM((Z, KB) + tile, BF16),
            pltpu.VMEM((KB, Z) + tile, BF16),
            pltpu.VMEM((Z, 8, BLK), jnp.int32),
            pltpu.SMEM((Z, 8, BLK), jnp.int32),
            pltpu.VMEM((FB, n, BLK), BF16),
            pltpu.VMEM((n, Z * BLK), BF16),
            pltpu.VMEM((Z, BLK, n), BF16),
            pltpu.VMEM((Z, n, BLK), F32),
            pltpu.VMEM((WIDTH, Z * BLK), BF16),
            pltpu.VMEM((WIDTH, Z * BLK), BF16),
            pltpu.VMEM((n, WIDTH), BF16),
            *token_buffers(),
            pltpu.VMEM((3, 8, BLK), F32),
            pltpu.VMEM((3, 8, BLK), F32),
            pltpu.VMEM((Q, 8, BLK), F32),
            pltpu.VMEM((FB, n, BLK), BF16),
            pltpu.VMEM((n, Z * BLK), BF16),
            pltpu.VMEM((n, WIDTH), BF16),
            pltpu.VMEM((Z, KB) + tile, BF16),
            pltpu.VMEM((Z, KB) + tile, BF16),
            *token_buffers(),
            pltpu.VMEM((KB, 2, 3) + tile, BF16),
            pltpu.VMEM((KB, 2, 4) + tile, BF16),
            pltpu.VMEM((KB,) + tile, BF16),
            pltpu.VMEM((3, Z) + tile, BF16),
            pltpu.VMEM((Z,) + tile, BF16),
            pltpu.VMEM((2, 3) + tile, BF16),
            pltpu.VMEM((2, 4) + tile, BF16),
            pltpu.VMEM(tile, BF16),
            pltpu.VMEM((X, Q, 16, BLK), BF16),
            pltpu.VMEM((Q, 16, BLK), BF16),
            pltpu.SemaphoreType.DMA((288,)),
            pltpu.SemaphoreType.DMA((288,)),
            pltpu.SemaphoreType.DMA((12,)),
        ],
        compiler_params=pltpu.CompilerParams(collective_id=0, has_side_effects=True, vmem_limit_bytes=46 << 20),
    )(*arrays)


def emit_kernel(*refs):
    sems = refs[-1]
    n = (len(refs) - 1) // 2
    copies = [pltpu.make_async_copy(refs[i], refs[n + i], sems.at[i]) for i in range(n)]
    for copy in copies:
        copy.start()
    for copy in copies:
        copy.wait()


def emit(*arrays):
    return pl.pallas_call(
        emit_kernel,
        name="emit",
        out_shape=tuple(jax.ShapeDtypeStruct(a.shape, a.dtype) for a in arrays),
        in_specs=[ANY] * len(arrays),
        out_specs=(pl.BlockSpec(memory_space=pltpu.HBM),) * len(arrays),
        scratch_shapes=[pltpu.SemaphoreType.DMA((len(arrays),))],
        compiler_params=pltpu.CompilerParams(vmem_limit_bytes=1 << 20),
    )(*arrays)


def on_device(
    inputs, norm_gain, w_in, w_out, block_index, segment_ids, teacher_scores, upstream, readout
):
    scale = 1.0 / math.sqrt(ROWS * X * Q * Z)
    remote = [pltpu.with_memory_space_constraint(a, pltpu.HBM)
              for a in (inputs, upstream, norm_gain[None, :], w_in, w_out, block_index.T,
                        segment_ids[None, :], teacher_scores[None, :], readout[None, :])]
    return emit(*step(scale, *remote))


def solution(mesh):
    return jax.shard_map(
        on_device,
        mesh=mesh,
        in_specs=(
            P(("tok", "feat"), None),
            P(),
            P("tok", "feat"),
            P("tok", "feat"),
            P("feat", None),
            P(("tok", "feat")),
            P(),
            P(("tok", "feat"), None),
            P(),
        ),
        out_specs=(
            P(("tok", "feat"), None),
            P(("tok", "feat"), None),
            P("tok", "feat"),
            P("tok", "feat"),
        ),
        check_vma=False,
    )
```

```python
import functools
import heapq
import math

import jax
import jax.numpy as jnp
from jax import lax
from jax.experimental import pallas as pl
from jax.experimental.pallas import tpu as pltpu
from jax.sharding import PartitionSpec as P

BLK = 128
EPS = 1e-06
LOSS_WEIGHT = 8.0
X, Y, C, Z = 4, 4, 2, 8
Q = Y * C
ROWS = 64
WIDTH = 2048
KB = 4
SEGMENTS = 1024
MESH = pl.DeviceIdType.MESH
F32, BF16 = jnp.float32, jnp.bfloat16
NT = (((1,), (1,)), ((), ()))
NN = (((1,), (0,)), ((), ()))
VM = pl.BlockSpec(memory_space=pltpu.VMEM)
ANY = pl.BlockSpec(memory_space=pl.ANY)


def dot(a, b, dims):
    return lax.dot_general(a, b, dims, preferred_element_type=F32)


class Place:
    def __init__(self):
        t = lax.axis_index("tok")
        self.z = lax.axis_index("feat")
        self.t = t
        self.q = lax.rem(t, Q)
        self.c = lax.rem(t, C)
        self.y = lax.rem(t // C, Y)
        self.x = t // Q

    def at(self, x=None, y=None, c=None, z=None):
        x, y = self.x if x is None else x, self.y if y is None else y
        c, z = self.c if c is None else c, self.z if z is None else z
        return {"tok": (x * Y + y) * C + c, "feat": z}

    def sibling(self):
        return self.at(c=1 - self.c)

    def along(self, axis, by):
        n = {"x": X, "y": Y, "z": Z}[axis]
        me = {"x": self.x, "y": self.y, "z": self.z}[axis]
        return self.at(**{axis: lax.rem(me + by + n, n)})

    def member(self, by):
        return {"tok": self.x * Q + lax.rem(self.q + by + Q, Q), "feat": self.z}

    def plane(self, dx, by):
        return {"tok": lax.rem(self.x + dx + X, X) * Q + lax.rem(self.q + by + Q, Q), "feat": self.z}

    def flat(self, by):
        n = X * Q * Z
        d = lax.rem(self.t * Z + self.z + by + n, n)
        return {"tok": d // Z, "feat": lax.rem(d, Z)}


class Mail:
    def __init__(self, send_sem, recv_sem):
        self.send_sem, self.recv_sem, self.sent = send_sem, recv_sem, []

    def send(self, src, dst, to):
        i = len(self.sent)
        copy = pltpu.make_async_remote_copy(
            src_ref=src,
            dst_ref=dst,
            send_sem=self.send_sem.at[i],
            recv_sem=self.recv_sem.at[i],
            device_id=to,
            device_id_type=MESH,
        )
        copy.start()
        self.sent.append(copy)
        return copy

    def close(self):
        for copy in self.sent:
            copy.wait_send()


def greet(devices, meanwhile=None):
    barrier = pltpu.get_barrier_semaphore()
    for device in devices:
        pl.semaphore_signal(barrier, inc=1, device_id=device, device_id_type=MESH)
    if meanwhile:
        meanwhile()
    pl.semaphore_wait(barrier, len(devices))


class Flows:
    def __init__(self):
        self.heap, self.now, self.count = [], 0.0, 0
        self.ended, self.pending = set(), []

    def add(self, flow, name=None):
        heapq.heappush(self.heap, (self.now, self.count, flow, name))
        self.count += 1

    def after(self, names, start):
        self.pending.append((set(names), start))

    def end(self, name):
        self.ended.add(name)
        for names, start in list(self.pending):
            if names <= self.ended:
                self.pending.remove((names, start))
                start()

    def run(self):
        while self.heap:
            self.now, _, flow, name = heapq.heappop(self.heap)
            for delay in flow:
                heapq.heappush(self.heap, (self.now + delay, self.count, flow, name))
                self.count += 1
                break
            else:
                if name is not None:
                    self.end(name)
        assert not self.pending


def gather_ring(mail, n, me, plus, minus, piece, half, delays, arrived=None):
    a = mail.send(piece(me), piece(me), plus)
    b = mail.send(piece(me), piece(me), minus)
    for step in range(1, n // 2 + 1):
        yield delays[step - 1]
        last = step == n // 2
        a.wait_recv()
        left = lax.rem(me - step + n, n)
        if not last:
            ref = half(left, 0) if step == n // 2 - 1 else piece(left)
            a = mail.send(ref, ref, plus)
            if arrived:
                arrived(left, None, n - step)
        elif arrived:
            arrived(left, 0, n - step)
        b.wait_recv()
        right = lax.rem(me + step, n)
        if not last:
            ref = half(right, 1) if step == n // 2 - 1 else piece(right)
            b = mail.send(ref, ref, minus)
            if arrived:
                arrived(right, None, step)
        elif arrived:
            arrived(right, 1, step)


def reduce_ring(mail, n, plus, minus, own, half, stage, land, delays, done):
    steps = n // 2
    a = mail.send(half(own(steps), 0), half(land(0, 1), 0), plus)
    b = mail.send(half(own(steps), 1), half(land(1, 1), 1), minus)
    for step in range(2, steps + 1):
        yield delays[step - 2]
        for way in (0, 1):
            mine = own(steps - step + 1 if way == 0 else n - steps + step - 1)
            (a, b)[way].wait_recv()
            came, out = land(way, step - 1), stage(way, step)
            if step == 2:
                half(out, way)[...] = (half(mine, way)[...].astype(F32) + half(came, way)[...].astype(F32)).astype(BF16)
                half(out, 1 - way)[...] = half(mine, 1 - way)[...]
            else:
                out[...] = (mine[...].astype(F32) + came[...].astype(F32)).astype(BF16)
            sent = mail.send(out, land(way, step), minus if way else plus)
            if way == 0:
                a = sent
            else:
                b = sent
    yield delays[steps - 1]
    mine = own(0)
    a.wait_recv()
    b.wait_recv()
    done(mine[...].astype(F32) + land(0, steps)[...].astype(F32) + land(1, steps)[...].astype(F32))


def halves(ref, h):
    return ref.at[pl.ds(h * 32, 32), :]


def reduce_tokens(mail, p, make, part, rs, pair, stage, land, done, times):
    other = 1 - p.c
    sends = {}
    ys = [lax.rem(p.y + o, Y) for o in range(Y)]
    for two in ((2, 1, 3, 0),):
        yield from make([ys[o] for o in two])
        for o in two:
            sends[o] = mail.send(part(ys[o] * C + other), rs.at[ys[o]], p.sibling())
        yield 0.2
    plus, minus = p.along("y", 1), p.along("y", -1)
    yield times[0]

    def fold(o):
        sends[o].wait_recv()
        pair[ys[o]] = (part(ys[o] * C + p.c)[...].astype(F32) + rs[ys[o]].astype(F32)).astype(BF16)

    fold(2)
    a = mail.send(halves(pair.at[ys[2]], 0), land.at[0, 0], plus)
    b = mail.send(halves(pair.at[ys[2]], 1), land.at[1, 0], minus)
    fold(1)
    a1 = mail.send(halves(pair.at[ys[1]], 1), land.at[0, 1], plus)
    fold(3)
    b1 = mail.send(halves(pair.at[ys[3]], 0), land.at[1, 1], minus)
    fold(0)
    yield times[1]
    a.wait_recv()
    stage[0] = (pair[ys[1], 0:32].astype(F32) + land[0, 0].astype(F32)).astype(BF16)
    a2 = mail.send(stage.at[0], land.at[0, 2], plus)
    b.wait_recv()
    stage[1] = (pair[ys[3], 32:64].astype(F32) + land[1, 0].astype(F32)).astype(BF16)
    b2 = mail.send(stage.at[1], land.at[1, 2], minus)
    yield times[2]
    for copy in (a1, b1, a2, b2):
        copy.wait_recv()
    top = pair[ys[0], 0:32].astype(F32) + land[0, 2].astype(F32) + land[1, 1].astype(F32)
    low = pair[ys[0], 32:64].astype(F32) + land[0, 1].astype(F32) + land[1, 2].astype(F32)
    done(jnp.concatenate([top, low], axis=0))


SQ = math.sqrt(2.0 / math.pi)
FAR_FIRST = (4, 3, 5, 2, 6, 1, 7, 0)
FB = WIDTH // BLK


def rows64(ref, h):
    return ref.at[pl.ds(h * 64, 64), :]


def step_kernel(scale, x_ref, up_ref, gain_ref, win_ref, wout_ref, bi_ref, seg_hbm, teacher_hbm, readout_hbm,
                lo_ref, ig_ref, gin_ref, gout_ref,
                x_v, gain_v, table_v, seg_ref, teacher_ref, readout_ref, nrm_all, up_all, win_all, wout_all, bi_all, bi,
                nrm_blocks, act_rows, act_t, slope, wide_out, wide_in, part,
                rs1, pair1, stage1, land1, ids, scores, coeffs,
                cot, pre, back, din, dout, rs, pair, stage, land,
                za_stage, za_land, za_sum, xb_land, xb_sum, zb_stage, zb_land,
                slab, dealt_in, dealt, send_sem, recv_sem, local_sem):
    p = Place()
    mail = Mail(send_sem, recv_sem)
    flows = Flows()
    local = []

    def keep(src, dst):
        copy = pltpu.make_async_copy(src, dst, local_sem.at[len(local)])
        copy.start()
        local.append(copy)
        return copy

    yplus, yminus = p.along("y", 1), p.along("y", -1)
    zplus, zminus = p.along("z", 1), p.along("z", -1)
    near = [p.flat(1), p.flat(-1)]
    eye = lax.broadcasted_iota(jnp.int32, (ROWS, BLK), 0) == lax.broadcasted_iota(jnp.int32, (ROWS, BLK), 1)
    loads = [keep(x_ref, x_v), keep(gain_ref, gain_v), keep(bi_ref, table_v), keep(seg_hbm, seg_ref),
             keep(teacher_hbm, teacher_ref), keep(readout_hbm, readout_ref), keep(up_ref, up_all.at[p.q])]

    def first():
        for copy in loads[:4]:
            copy.wait()
        wide = x_v[...].astype(F32)
        inv_rms = lax.rsqrt(jnp.mean(wide * wide, axis=1, keepdims=True) + EPS)
        nrm_all[p.q] = (wide * inv_rms * gain_v[...]).astype(BF16)
        bi_all[p.z] = jnp.zeros((8, BLK), jnp.int32)
        bi_all[p.z, 0:KB, 0:Z] = table_v[...]
        ids[0] = jnp.full((8, BLK), -1.0, F32)
        ids[0, 0:1, 0:ROWS] = seg_ref[...].astype(F32)
        for copy in loads[4:]:
            copy.wait()

    greet([p.plane(dx, o) for dx in range(X) for o in range(Q) if dx or o] + [zplus, zminus] + near, first)
    id_copies = [mail.send(ids.at[0], ids.at[1 + i], near[i]) for i in (0, 1)]

    def columns(ref, q):
        return ref.at[:, pl.ds(pl.multiple_of(q * BLK, BLK), BLK)]

    def my_rows(ref):
        return ref.at[pl.ds(pl.multiple_of(p.q * 16, 16), 16), :]

    in_slab, out_slab = win_all.at[p.z, p.x], wout_all.at[p.x, p.z]
    in_deals, out_deals = {}, []
    for o in range(Q):
        q = lax.rem(p.q + o, Q)
        for dx in range(X):
            if dx or o:
                in_deals[dx, o] = mail.send(columns(win_ref, q), my_rows(in_slab), p.plane(dx, o))
        if o:
            out_deals.append(mail.send(columns(wout_ref, q), my_rows(out_slab), p.member(o)))
    slab_copies = [keep(columns(win_ref, p.q), my_rows(in_slab)), keep(columns(wout_ref, p.q), my_rows(out_slab))]

    def tokens(out, first):
        def half(y, h):
            return out.at[y * C + p.c, pl.ds(h * 32, 32), :]

        relays = []

        def pass_on(ref, to):
            relays.append(mail.send(ref, ref, to))
            return relays[-1]

        a0 = mail.send(half(p.y, 0), half(p.y, 0), yplus)
        b1 = mail.send(half(p.y, 1), half(p.y, 1), yminus)
        a1 = mail.send(half(p.y, 1), half(p.y, 1), yplus)
        b0 = mail.send(half(p.y, 0), half(p.y, 0), yminus)
        pass_on(out.at[p.q], p.sibling())
        left, right, far = lax.rem(p.y + 3, Y), lax.rem(p.y + 1, Y), lax.rem(p.y + 2, Y)
        yield first
        a0.wait_recv()
        fa = mail.send(half(left, 0), half(left, 0), yplus)
        pass_on(half(left, 0), p.sibling())
        b1.wait_recv()
        fb = mail.send(half(right, 1), half(right, 1), yminus)
        pass_on(half(right, 1), p.sibling())
        yield 3.0
        a1.wait_recv()
        pass_on(half(left, 1), p.sibling())
        b0.wait_recv()
        pass_on(half(right, 0), p.sibling())
        yield 8.3
        fa.wait_recv()
        pass_on(half(far, 0), p.sibling())
        fb.wait_recv()
        pass_on(half(far, 1), p.sibling())
        yield 2.0
        for copy in relays:
            copy.wait_recv()

    def table():
        mine = bi_all.at[p.z]
        a = mail.send(mine, mine, zplus)
        b = mail.send(mine, mine, zminus)
        for step in range(1, Z // 2 + 1):
            yield 2.5
            a.wait_recv()
            left = bi_all.at[lax.rem(p.z - step + Z, Z)]
            if step < Z // 2:
                a = mail.send(left, left, zplus)
                b.wait_recv()
                right = bi_all.at[lax.rem(p.z + step, Z)]
                if step < Z // 2 - 1:
                    b = mail.send(right, right, zminus)
        known = pltpu.make_async_copy(bi_all, bi, local_sem.at[11])
        known.start()
        known.wait()

    arrivals = {}

    def got_in(z, h, d):
        arrivals[d] = arrivals.get(d, 0) + 1
        if arrivals[d] == (KB if h is None else 2 * KB):
            flows.end(("w_in", d))

    def w_in_z(k):
        return gather_ring(
            mail, Z, p.z, zplus, zminus,
            lambda z: win_all.at[z, k],
            lambda z, h: win_all.at[z, k, pl.ds(h * 64, 64), :],
            [3.0] * 4, got_in)

    def w_out_x(z):
        ref = wout_all.at[p.x, z]
        copies = [mail.send(ref, ref, p.along("x", dx)) for dx in (1, 2, 3)]
        yield 6.0
        for copy in copies:
            copy.wait_recv()

    def w_in():
        yield 2.5
        slab_copies[0].wait()
        for dx in range(X):
            for o in range(Q):
                if dx or o:
                    in_deals[dx, o].wait_recv()
            flows.add(w_in_z(lax.rem(p.x - dx + X, X)))
            yield 0.3
        flows.end(("w_in", 0))

    def w_out():
        yield 2.6
        slab_copies[1].wait()
        for copy in out_deals:
            copy.wait_recv()
        seen = []

        def got(z, h, d):
            if h is not None:
                seen.append(h)
            if h is None or len(seen) == 2:
                flows.add(w_out_x(z), ("w_out", d))

        flows.add(gather_ring(
            mail, Z, p.z, zplus, zminus,
            lambda z: wout_all.at[p.x, z],
            lambda z, h: wout_all.at[p.x, z, pl.ds(h * 64, 64), :],
            [2.5] * 4, got))
        flows.add(w_out_x(p.z), ("w_out", 0))


    def member_rows(y):
        return pl.ds(pl.multiple_of(y * (C * ROWS), C * ROWS), C * ROWS)

    def member(ref):
        return lambda q: ref.at[pl.ds(pl.multiple_of(q * ROWS, ROWS), ROWS), :]

    def widen(j, blocks, out):
        at = [bi[lax.rem(p.z + j, Z), k, p.q] for k in range(KB)]
        cols = slice(j * BLK, (j + 1) * BLK)
        for d in range(FB):
            out[d * BLK:(d + 1) * BLK, cols] = sum(
                blocks[k] * (at[k] == d).astype(F32).astype(BF16) for k in range(KB))

    def product(lhs, wide, out):
        def make(ys):
            rows = jnp.concatenate([lhs[member_rows(y), :] for y in ys], axis=0)
            for n in range(4):
                cols = slice(n * 512, (n + 1) * 512)
                value = dot(rows, wide[cols, :], NT).astype(BF16)
                for i, y in enumerate(ys):
                    out[member_rows(y), cols] = value[i * C * ROWS:(i + 1) * C * ROWS]
                yield 0.5
        return make

    total = []

    def blocks():
        for d in range(FB):
            nrm_blocks[d] = nrm_all[:, :, d * BLK:(d + 1) * BLK].reshape(Q * ROWS, BLK)
        yield 0.3

    def forward_block(d):
        j = lax.rem(p.z + d, Z)
        at = [bi[j, k, p.q] for k in range(KB)]
        picked = jnp.concatenate([nrm_blocks[a] for a in at], axis=1)
        v = dot(picked, win_all[j].reshape(KB * BLK, BLK), NN)
        tanh = jnp.tanh(SQ * (v + 0.044715 * (v * v * v)))
        act = 0.5 * v * (1.0 + tanh)
        slope[d] = 0.5 * (1.0 + tanh) + 0.5 * v * (1.0 - tanh * tanh) * (SQ * (1.0 + 3.0 * 0.044715 * (v * v)))
        act_rows[:, d * BLK:(d + 1) * BLK] = act.astype(BF16)
        act_t[d] = act.T.astype(BF16)
        yield 0.5
        widen(d, [wout_all[k, j] for k in range(KB)], wide_out)
        yield 0.3

    def forward():
        yield from reduce_tokens(
            mail, p, product(act_rows, wide_out, part), member(part), rs1, pair1, stage1, land1,
            total.append, [1.0, 4.0, 4.0])

    def wide_weights():
        yield 4.5
        for d in range(Z):
            widen(d, [win_all[lax.rem(p.z + d, Z), k] for k in range(KB)], wide_in)
            yield 0.4

    def score():
        lo = (x_v[...].astype(F32) + total[0]).astype(BF16)
        lo_ref[...] = lo
        token = jnp.sum(lo.astype(F32) * readout_ref[...], axis=1, keepdims=True)
        scores[0] = jnp.broadcast_to(jnp.sum(jnp.where(eye, token, 0.0), axis=0, keepdims=True), (8, BLK))
        copies = [mail.send(scores.at[0], scores.at[1 + i], near[i]) for i in (0, 1)]
        ids_col = jnp.sum(jnp.where(eye, ids[0, 0:1, :], 0.0), axis=1, keepdims=True)
        segs = teacher_ref.shape[1]
        hot = lax.broadcasted_iota(jnp.int32, (ROWS, segs), 1).astype(F32) == ids_col
        teacher = jnp.sum(jnp.where(hot, teacher_ref[...], 0.0), axis=1, keepdims=True)
        yield 2.5
        for copy in id_copies + copies:
            copy.wait_recv()
        sums = jnp.zeros((ROWS, 1), F32)
        counts = jnp.zeros((ROWS, 1), F32)
        for i in range(3):
            same = ids[i, 0:1, :] == ids_col
            sums += jnp.sum(jnp.where(same, scores[i, 0:1, :], 0.0), axis=1, keepdims=True)
            counts += jnp.sum(jnp.where(same, 1.0, 0.0), axis=1, keepdims=True)
        coeff = (2.0 * LOSS_WEIGHT) * (sums / counts - teacher)
        coeff_row = jnp.sum(jnp.where(eye, coeff, 0.0), axis=0, keepdims=True)
        coeffs[p.q] = jnp.broadcast_to(coeff_row, (8, BLK))
        out = [mail.send(coeffs.at[p.q], coeffs.at[p.q], p.member(o)) for o in range(1, Q)]
        yield 2.5
        for copy in out:
            copy.wait_recv()

    def cotangent(b):
        coeff = jnp.sum(jnp.where(eye, coeffs[b][0:1, :], 0.0), axis=1, keepdims=True)
        return (up_all[b].astype(F32) + coeff * readout_ref[...]).astype(BF16)

    def block(dz):
        j = lax.rem(p.z + dz, Z)
        at = [bi[j, k, p.q] for k in range(KB)]
        picked = jnp.concatenate([cot[a] for a in at], axis=1)
        chosen = jnp.concatenate([nrm_blocks[a] for a in at], axis=1)
        w_out = jnp.concatenate([wout_all[k, j] for k in range(KB)], axis=0)
        value = dot(picked, w_out, NN) * slope[dz]
        pre[:, dz * BLK:(dz + 1) * BLK] = value.astype(BF16)
        yield 0.4
        d_in = (dot(value.T.astype(BF16), chosen, NN) * scale).astype(BF16)
        yield 0.3
        d_out = (dot(act_t[dz], picked, NN) * scale).astype(BF16)
        for k in range(KB):
            cols = slice(k * BLK, (k + 1) * BLK)
            din[dz, k] = d_in[:, cols]
            dout[dz, k] = d_out[:, cols]

    ready = set()
    grads, deals, x_sends = [], [], {}

    def out_x(dz):
        for dx in (1, 2, 3):
            x = lax.rem(p.x + dx, X)
            x_sends[dz, dx] = mail.send(dout.at[dz, x], xb_land.at[dx - 1, dz], p.along("x", dx))

    def in_z(dx):
        k = lax.rem(p.x + dx, X)

        def own(dz):
            assert dz in ready
            return din.at[dz, k]

        def done(value):
            za_sum[dx] = value.T.astype(BF16)
            for o in range(Q):
                rows = pl.ds(pl.multiple_of(lax.rem(p.q + o, Q) * 16, 16), 16)
                if dx == 0 and o == 0:
                    dealt_in[p.x, p.q] = za_sum[dx, rows, :]
                else:
                    deals.append(mail.send(za_sum.at[dx, rows, :], dealt_in.at[p.x, p.q], p.plane(dx, o)))

        return reduce_ring(
            mail, Z, zplus, zminus, own, rows64,
            lambda way, step: za_stage.at[dx, way, step - 2], lambda way, step: za_land.at[dx, way, step - 1],
            [4.5] * 4, done)

    summed = set()

    def out_own(dz):
        if dz not in summed:
            assert dz in ready
            summed.add(dz)
            for dx in (1, 2, 3):
                x_sends[dz, dx].wait_recv()
            value = dout[dz, p.x].astype(F32) + sum(xb_land[i, dz].astype(F32) for i in range(3))
            xb_sum[dz] = value.astype(BF16)
        return xb_sum.at[dz]

    def deal(value):
        slab[...] = value.T.astype(BF16)
        dealt[p.q] = slab[pl.ds(pl.multiple_of(p.q * 16, 16), 16), :]
        for o in range(1, Q):
            rows = slab.at[pl.ds(pl.multiple_of(lax.rem(p.q + o, Q) * 16, 16), 16), :]
            deals.append(mail.send(rows, dealt.at[p.q], p.member(o)))

    def out_z():
        yield 3.5
        yield from reduce_ring(
            mail, Z, zplus, zminus, out_own, rows64,
            lambda way, step: zb_stage.at[way, step - 2], lambda way, step: zb_land.at[way, step - 1],
            [4.0] * 4, deal)

    def compute():
        for b in range(Q):
            value = cotangent(b)
            for d in range(FB):
                cot[d, b * ROWS:(b + 1) * ROWS, :] = value[:, d * BLK:(d + 1) * BLK]
        for dz in FAR_FIRST:
            yield from block(dz)
            ready.add(dz)
            out_x(dz)
            if dz == FAR_FIRST[0]:
                for dx in (1, 2, 3, 0):
                    flows.add(in_z(dx))
                flows.add(out_z())
            yield 0.3
        yield from reduce_tokens(
            mail, p, product(pre, wide_in, back), member(back), rs, pair, stage, land,
            grads.append, [1.0, 6.5, 8.0])

    flows.add(w_in())
    flows.add(w_out())
    flows.add(tokens(nrm_all, 4.5), "normed")
    flows.add(tokens(up_all, 14.0), "upstream")
    flows.add(table(), "table")
    flows.after(["normed"], lambda: flows.add(blocks(), "blocks"))
    for d in range(Z):
        flows.after(["blocks", "table", ("w_in", d), ("w_out", d)],
                    lambda d=d: flows.add(forward_block(d), ("act", d)))
    flows.after([("act", d) for d in range(Z)],
                lambda: (flows.add(forward(), "forward"), flows.add(wide_weights(), "wide")))
    flows.after(["forward"], lambda: flows.add(score(), "score"))
    flows.after(["score", "upstream", "wide"], lambda: flows.add(compute()))
    flows.run()

    wide = x_v[...].astype(F32)
    inv = lax.rsqrt(jnp.mean(wide * wide, axis=1, keepdims=True) + EPS)
    scaled = grads[0] * gain_v[...]
    inner = jnp.mean(scaled * wide, axis=1, keepdims=True)
    ig_ref[...] = (cotangent(p.q).astype(F32) + (inv * scaled - wide * (inv * inv * inv) * inner)).astype(BF16)
    for copy in deals:
        copy.wait_recv()
    for q in range(Q):
        cols = slice(q * BLK, (q + 1) * BLK)
        gin_ref[:, cols] = sum(dealt_in[x, q].astype(F32) for x in range(X))
        gout_ref[:, cols] = dealt[q].astype(F32)
    mail.close()


def step(scale, *arrays):
    n = Q * ROWS
    tile = (BLK, BLK)
    far = pl.BlockSpec(memory_space=pltpu.HBM)

    def token_buffers():
        return [
            pltpu.VMEM((Y, ROWS, WIDTH), BF16),
            pltpu.VMEM((Y, ROWS, WIDTH), BF16),
            pltpu.VMEM((2, ROWS // 2, WIDTH), BF16),
            pltpu.VMEM((2, 3, ROWS // 2, WIDTH), BF16),
        ]

    return pl.pallas_call(
        functools.partial(step_kernel, scale),
        name="step",
        out_shape=(
            jax.ShapeDtypeStruct((ROWS, WIDTH), BF16),
            jax.ShapeDtypeStruct((ROWS, WIDTH), BF16),
            jax.ShapeDtypeStruct((16, Q * BLK), F32),
            jax.ShapeDtypeStruct((16, Q * BLK), F32),
        ),
        in_specs=[far] * 9,
        out_specs=(VM,) * 4,
        scratch_shapes=[
            pltpu.VMEM((ROWS, WIDTH), BF16),
            pltpu.VMEM((1, WIDTH), F32),
            pltpu.VMEM((KB, Z), jnp.int32),
            pltpu.VMEM((1, ROWS), jnp.int32),
            pltpu.VMEM((1, SEGMENTS), F32),
            pltpu.VMEM((1, WIDTH), F32),
            pltpu.VMEM((Q, ROWS, WIDTH), BF16),
            pltpu.VMEM((Q, ROWS, WIDTH), BF16),
            pltpu.VMEM((Z, KB) + tile, BF16),
            pltpu.VMEM((KB, Z) + tile, BF16),
            pltpu.VMEM((Z, 8, BLK), jnp.int32),
            pltpu.SMEM((Z, 8, BLK), jnp.int32),
            pltpu.VMEM((FB, n, BLK), BF16),
            pltpu.VMEM((n, Z * BLK), BF16),
            pltpu.VMEM((Z, BLK, n), BF16),
            pltpu.VMEM((Z, n, BLK), F32),
            pltpu.VMEM((WIDTH, Z * BLK), BF16),
            pltpu.VMEM((WIDTH, Z * BLK), BF16),
            pltpu.VMEM((n, WIDTH), BF16),
            *token_buffers(),
            pltpu.VMEM((3, 8, BLK), F32),
            pltpu.VMEM((3, 8, BLK), F32),
            pltpu.VMEM((Q, 8, BLK), F32),
            pltpu.VMEM((FB, n, BLK), BF16),
            pltpu.VMEM((n, Z * BLK), BF16),
            pltpu.VMEM((n, WIDTH), BF16),
            pltpu.VMEM((Z, KB) + tile, BF16),
            pltpu.VMEM((Z, KB) + tile, BF16),
            *token_buffers(),
            pltpu.VMEM((KB, 2, 3) + tile, BF16),
            pltpu.VMEM((KB, 2, 4) + tile, BF16),
            pltpu.VMEM((KB,) + tile, BF16),
            pltpu.VMEM((3, Z) + tile, BF16),
            pltpu.VMEM((Z,) + tile, BF16),
            pltpu.VMEM((2, 3) + tile, BF16),
            pltpu.VMEM((2, 4) + tile, BF16),
            pltpu.VMEM(tile, BF16),
            pltpu.VMEM((X, Q, 16, BLK), BF16),
            pltpu.VMEM((Q, 16, BLK), BF16),
            pltpu.SemaphoreType.DMA((288,)),
            pltpu.SemaphoreType.DMA((288,)),
            pltpu.SemaphoreType.DMA((12,)),
        ],
        compiler_params=pltpu.CompilerParams(collective_id=0, has_side_effects=True, vmem_limit_bytes=46 << 20),
    )(*arrays)


def emit_kernel(*refs):
    sems = refs[-1]
    n = (len(refs) - 1) // 2
    copies = [pltpu.make_async_copy(refs[i], refs[n + i], sems.at[i]) for i in range(n)]
    for copy in copies:
        copy.start()
    for copy in copies:
        copy.wait()


def emit(*arrays):
    return pl.pallas_call(
        emit_kernel,
        name="emit",
        out_shape=tuple(jax.ShapeDtypeStruct(a.shape, a.dtype) for a in arrays),
        in_specs=[ANY] * len(arrays),
        out_specs=(pl.BlockSpec(memory_space=pltpu.HBM),) * len(arrays),
        scratch_shapes=[pltpu.SemaphoreType.DMA((len(arrays),))],
        compiler_params=pltpu.CompilerParams(vmem_limit_bytes=1 << 20),
    )(*arrays)


def on_device(
    inputs, norm_gain, w_in, w_out, block_index, segment_ids, teacher_scores, upstream, readout
):
    scale = 1.0 / math.sqrt(ROWS * X * Q * Z)
    remote = [pltpu.with_memory_space_constraint(a, pltpu.HBM)
              for a in (inputs, upstream, norm_gain[None, :], w_in, w_out, block_index.T,
                        segment_ids[None, :], teacher_scores[None, :], readout[None, :])]
    return emit(*step(scale, *remote))


def solution(mesh):
    return jax.shard_map(
        on_device,
        mesh=mesh,
        in_specs=(
            P(("tok", "feat"), None),
            P(),
            P("tok", "feat"),
            P("tok", "feat"),
            P("feat", None),
            P(("tok", "feat")),
            P(),
            P(("tok", "feat"), None),
            P(),
        ),
        out_specs=(
            P(("tok", "feat"), None),
            P(("tok", "feat"), None),
            P("tok", "feat"),
            P("tok", "feat"),
        ),
        check_vma=False,
    )
```
